768 devices in a mesh: shell: 96 (over x, z, core), atom: 8 (over y).
Axes of the slice: x: 4, y: 8, z: 12, core: 2. Of those that a mesh axis runs over, the one named last changes fastest.
Arguments:
- rho: float32 [393216], P('shell'), may hold values from 0.5 to 1.5
- task_point: int32 [96, 768, 256], P('shell', 'atom'), may hold values from 0 to 4095
- task_count: int32 [96, 768], P('shell', 'atom'), may hold values from 1 to 256
- radial_index: int32 [96, 768, 256], P('shell', 'atom'), may hold values from 0 to 126
- fraction: float32 [96, 768, 256], P('shell', 'atom'), may hold values from 0 to 1
- angular: bfloat16 [96, 768, 49, 256], P('shell', 'atom'), may hold values from -6 to 6
- green: float32 [7, 128, 128], replicated, may hold values from -0.0017089844 to 0.0017089844
Outputs:
- potential: float32 [393216], P(('shell', 'atom'))
The draws below stay inside these ranges and needn't reach their ends.
Inputs may be any that keep to these rules, and one draw needn't show every extreme that they name: Slots j with j >= task_count of their atom and batch are unused.
All inputs are finite; a program needn't handle non-finite values.
Results may differ from the reference program's by a relative error of at most 0.005.
Values may be sent and summed in bfloat16 or wider, within the bound.
No kernel may reach another device: no remote copies, remote signals or barrier semaphores. Data moves between devices by JAX's collectives and lax.ppermute only.
A program may use at most 32 MiB of HBM per device.

```python
import math
import jax
import jax.numpy as jnp
import numpy as np
from jax import lax

LMAX = 6
LM = 49
R = 128
SLOTS = 256
PTS = 4096
ATOMS = 768
NPTS = 393216
N_SHELL = 96
N_ATOM = 8


def with_ends(drawn, stream_key, smallest, largest):
    spot = [jax.random.randint(jax.random.fold_in(stream_key, axis), (), 0, length) for axis, length in enumerate(drawn.shape)]
    longest = drawn.shape.index(max(drawn.shape))
    neighbour = spot[:longest] + [(spot[longest] + 1) % drawn.shape[longest]] + spot[longest + 1:]
    return drawn.at[tuple(spot)].set(smallest).at[tuple(neighbour)].set(largest)


def shard_levels(own_key, dims, shards, least, high):
    def one(axis_at, parts):
        heights = jax.random.uniform(jax.random.fold_in(jax.random.fold_in(own_key, 6), axis_at), (parts,), jnp.float32, least / len(shards), high / len(shards))
        return jnp.repeat(jnp.exp(heights), dims[axis_at] // parts).reshape((-1,) + (1,) * (len(dims) - axis_at - 1))

    factor_of = one(*shards[0])
    for cut in shards[1:]:
        factor_of = factor_of * one(*cut)
    return factor_of


def scatter_about(stream_key, extent, deviation, limit, cuts=(), held_as=jnp.bfloat16):
    result = jax.random.normal(stream_key, extent, jnp.float32) * deviation
    if len(cuts) > 0:
        result = shard_levels(stream_key, extent, cuts, -0.22, 0.18) * result
    return jnp.clip(result, min=-limit, max=limit).astype(held_as)


def setup_inputs(seed: int = 0) -> dict:
    streams_of = jax.random.split(jax.random.key(seed), 8)
    rho = jnp.clip(0.5 + 1.0 * jax.random.uniform(streams_of[0], (NPTS,), jnp.float32) ** shard_levels(streams_of[0], (NPTS,), ((0, 96),), -0.2, 0.2), 0.5, 1.5)
    task_point = with_ends(jax.random.randint(streams_of[1], (N_SHELL, ATOMS, SLOTS), 0, PTS), jax.random.fold_in(streams_of[1], 1), 0, PTS - 1).astype(jnp.int32)
    task_count = with_ends(jax.random.randint(streams_of[2], (N_SHELL, ATOMS), 1, SLOTS + 1), jax.random.fold_in(streams_of[2], 1), 1, SLOTS).astype(jnp.int32)
    radial_index = with_ends(jax.random.randint(streams_of[3], (N_SHELL, ATOMS, SLOTS), 0, R - 1), jax.random.fold_in(streams_of[3], 1), 0, (R - 1) - 1).astype(jnp.int32)
    fraction = jnp.clip(1.0 * jax.random.uniform(streams_of[4], (N_SHELL, ATOMS, SLOTS), jnp.float32) ** shard_levels(streams_of[4], (N_SHELL, ATOMS, SLOTS), ((0, 96), (1, 8)), -0.2, 0.2), 0.0, 1.0)
    angular = scatter_about(streams_of[5], (N_SHELL, ATOMS, LM, SLOTS), 1.0, 6.0, ((0, 96), (1, 8)))
    green = scatter_about(streams_of[6], (LMAX + 1, R, R), (12 * SLOTS * SLOTS * N_SHELL * N_SHELL * N_ATOM // PTS) ** -0.5, 0.0017089844, (), jnp.float32)
    return {"rho": rho, "task_point": task_point, "task_count": task_count, "radial_index": radial_index, "fraction": fraction, "angular": angular, "green": green}


def degree_table():
    return np.array([int(math.isqrt(i)) for i in range(LM)], dtype=np.int32)

def radial_rows(radial_index, fraction):
    grid = jnp.arange(R, dtype=jnp.int32)
    lower = (grid == radial_index[..., None]).astype(jnp.float32) * (1.0 - fraction)[..., None]
    upper = (grid == radial_index[..., None] + 1).astype(jnp.float32) * fraction[..., None]
    return (lower + upper).astype(jnp.bfloat16)

def reference(rho, task_point, task_count, radial_index, fraction, angular, green):
    density = rho.reshape(N_SHELL, PTS)
    slot_ids = jnp.arange(SLOTS, dtype=jnp.int32)

    def batch_terms(batch):
        live = (slot_ids[None, :] < task_count[batch][:, None]).astype(jnp.float32)
        picked = density[batch][task_point[batch]] * live
        weighted = (angular[batch].astype(jnp.float32) * picked[:, None, :]).astype(jnp.bfloat16)
        rows = radial_rows(radial_index[batch], fraction[batch])
        return (live, weighted, rows)

    def accumulate(batch, total):
        live, weighted, rows = batch_terms(batch)
        return total + jnp.einsum('als,asr->alr', weighted.astype(jnp.float32), rows.astype(jnp.float32), precision=lax.Precision.HIGHEST)
    moments = lax.fori_loop(0, N_SHELL, accumulate, jnp.zeros((ATOMS, LM, R), jnp.float32))
    kernels = green[degree_table()]
    table = jnp.einsum('alq,lqr->alr', moments, kernels, precision=lax.Precision.HIGHEST).astype(jnp.bfloat16)

    def evaluate(batch):
        live, weighted, rows = batch_terms(batch)
        radial = jnp.einsum('alr,asr->als', table.astype(jnp.float32), rows.astype(jnp.float32), precision=lax.Precision.HIGHEST)
        values = lax.optimization_barrier(jnp.sum(angular[batch].astype(jnp.float32) * radial, axis=1)) * live
        return jnp.zeros((PTS,), jnp.float32).at[task_point[batch].reshape(-1)].add(values.reshape(-1))
    potential = lax.map(evaluate, jnp.arange(N_SHELL, dtype=jnp.int32))
    return potential.reshape(N_SHELL * PTS)
```

```python
import jax
import jax.numpy as jnp
from jax import lax
from jax.experimental import pallas as pl
from jax.experimental.pallas import tpu as pltpu
from jax.sharding import Mesh, PartitionSpec as P

X, Z, CORES = 4, 12, 2
LMAX = 6
LM = 49
ROWS = 56
R = 128
SLOTS = 256
PTS = 4096
HALF = 48
BLOCK = 8
STEPS = HALF // BLOCK
HIGH, LOW = 32, 128

f32 = jnp.float32
bf16 = jnp.bfloat16


def hat_rows(index, fraction):
    grid = lax.broadcasted_iota(jnp.int32, (R, SLOTS), 0)
    upper = jnp.where(grid == index + 1, fraction, 0.0)
    return jnp.where(grid == index, 1.0 - fraction, upper).astype(bf16)


def one_hot_low(points):
    grid = lax.broadcasted_iota(jnp.int32, (LOW, SLOTS), 0)
    return jnp.where(grid == (points & (LOW - 1)), 1.0, 0.0).astype(bf16)


def is_high(points):
    return lax.broadcasted_iota(jnp.int32, (HIGH, SLOTS), 0) == lax.shift_right_logical(points, 7)


def moments_kernel(half_ref, count_ref, rho_ref, point_ref, index_ref, fraction_ref, angular_ref, out_ref, weighted_ref):
    first = (half_ref[0] * STEPS + pl.program_id(0)) * BLOCK
    rho = rho_ref[...]
    big = rho.astype(bf16)
    small = (rho - big.astype(f32)).astype(bf16)
    rho_parts = jnp.concatenate([big, small], axis=1)
    slot = lax.broadcasted_iota(jnp.int32, (1, SLOTS), 1)
    densities = []
    for i in range(BLOCK):
        points = point_ref[i : i + 1, :]
        low = one_hot_low(points)
        columns = jnp.dot(rho_parts, jnp.concatenate([low, low], axis=0), preferred_element_type=f32)
        picked = jnp.sum(jnp.where(is_high(points), columns, 0.0), axis=0, keepdims=True)
        densities.append(jnp.where(slot < count_ref[first + i], picked, 0.0))
    densities = jnp.concatenate(densities, axis=0)
    for m in range(LM):
        weighted_ref[m] = angular_ref[m].astype(f32) * densities
    weighted_ref[LM:] = jnp.zeros((ROWS - LM, BLOCK, SLOTS), f32)
    for i in range(BLOCK):
        rows = hat_rows(index_ref[i : i + 1, :], fraction_ref[i : i + 1, :])
        out_ref[i] = lax.dot_general(
            weighted_ref[:, i, :].astype(bf16), rows, (((1,), (1,)), ((), ())), preferred_element_type=f32
        ).astype(bf16)


def evaluate_kernel(half_ref, count_ref, table_ref, point_ref, index_ref, fraction_ref, angular_ref, out_ref, sum_ref, radial_ref):
    first = (half_ref[0] * STEPS + pl.program_id(0)) * BLOCK
    slot = lax.broadcasted_iota(jnp.int32, (1, SLOTS), 1)

    @pl.when(pl.program_id(0) == 0)
    def _():
        sum_ref[...] = jnp.zeros_like(sum_ref)

    for i in range(BLOCK):
        rows = hat_rows(index_ref[i : i + 1, :], fraction_ref[i : i + 1, :])
        radial_ref[:, i, :] = jnp.dot(table_ref[i], rows, preferred_element_type=f32)
    values = angular_ref[0].astype(f32) * radial_ref[0]
    for m in range(1, LM):
        values = values + angular_ref[m].astype(f32) * radial_ref[m]
    total = sum_ref[...]
    for i in range(BLOCK):
        points = point_ref[i : i + 1, :]
        value = jnp.where(slot < count_ref[first + i], values[i : i + 1, :], 0.0)
        big = value.astype(bf16).astype(f32)
        small = value - big
        high = is_high(points)
        spread = jnp.concatenate([jnp.where(high, big, 0.0), jnp.where(high, small, 0.0)], axis=0)
        total = total + lax.dot_general(
            spread.astype(bf16), one_hot_low(points), (((1,), (1,)), ((), ())), preferred_element_type=f32
        )
    sum_ref[...] = total

    @pl.when(pl.program_id(0) == STEPS - 1)
    def _():
        out_ref[...] = total[:HIGH] + total[HIGH:]


def solve_kernel(parts_ref, green_ref, table_ref):
    moments = jnp.sum(parts_ref[...].astype(f32), axis=0)
    row = lax.broadcasted_iota(jnp.int32, (ROWS, R), 0)
    table = jnp.zeros((ROWS, R), f32)
    for degree in range(LMAX + 1):
        of_degree = (row >= degree * degree) & (row < (degree + 1) * (degree + 1))
        table = table + jnp.dot(
            jnp.where(of_degree, moments, 0.0), green_ref[degree], precision=lax.Precision.HIGHEST, preferred_element_type=f32
        )
    table_ref[...] = table.astype(bf16)


def task_block(half_of):
    return pl.BlockSpec((BLOCK, SLOTS), lambda step, half, count: (half[0] * STEPS + step, 0))


def angular_block():
    return pl.BlockSpec((LM, BLOCK, SLOTS), lambda step, half, count: (0, half[0] * STEPS + step, 0))


def moments_of(half, count, rho, points, index, fraction, angular):
    return pl.pallas_call(
        moments_kernel,
        out_shape=jax.ShapeDtypeStruct((HALF, ROWS, R), bf16),
        grid_spec=pltpu.PrefetchScalarGridSpec(
            num_scalar_prefetch=2,
            grid=(STEPS,),
            in_specs=[pl.BlockSpec((HIGH, LOW), lambda step, half, count: (0, 0))]
            + [task_block(half)] * 3
            + [angular_block()],
            out_specs=pl.BlockSpec((BLOCK, ROWS, R), lambda step, half, count: (step, 0, 0)),
            scratch_shapes=[pltpu.VMEM((ROWS, BLOCK, SLOTS), f32)],
        ),
        name="moments",
    )(half, count, rho, points, index, fraction, angular)


def evaluated(half, count, table, points, index, fraction, angular):
    return pl.pallas_call(
        evaluate_kernel,
        out_shape=jax.ShapeDtypeStruct((HIGH, LOW), f32),
        grid_spec=pltpu.PrefetchScalarGridSpec(
            num_scalar_prefetch=2,
            grid=(STEPS,),
            in_specs=[pl.BlockSpec((BLOCK, ROWS, R), lambda step, half, count: (step, 0, 0))]
            + [task_block(half)] * 3
            + [angular_block()],
            out_specs=pl.BlockSpec((HIGH, LOW), lambda step, half, count: (0, 0)),
            scratch_shapes=[pltpu.VMEM((2 * HIGH, LOW), f32), pltpu.VMEM((ROWS, BLOCK, SLOTS), f32)],
        ),
        name="evaluate",
    )(half, count, table, points, index, fraction, angular)


def solved(parts, green):
    return pl.pallas_call(
        solve_kernel,
        out_shape=jax.ShapeDtypeStruct((ROWS, R), bf16),
        name="solve",
    )(parts, green)


def exchanged(array, axis):
    return lax.all_to_all(array, axis, split_axis=0, concat_axis=0, tiled=True)


def to_other_core(array):
    return lax.ppermute(array, "core", [(0, 1), (1, 0)])


def per_device(rho, task_point, task_count, radial_index, fraction, angular, green):
    core = lax.axis_index("core")
    own = core.astype(jnp.int32).reshape(1)
    other = 1 - own
    tasks = (task_point[0], radial_index[0], fraction[0], angular[0].transpose(1, 0, 2))
    count = task_count[0]
    rho = rho.reshape(HIGH, LOW)

    sent = moments_of(other, count, rho, *tasks)
    arrived = to_other_core(sent)
    kept = moments_of(own, count, rho, *tasks)
    chip = (kept.astype(f32) + arrived.astype(f32)).astype(bf16)
    along_x = exchanged(chip.reshape(X, Z, ROWS, R), "x")
    plane = along_x.astype(f32).sum(axis=0).astype(bf16)
    parts = exchanged(plane, "z")
    table = solved(parts, green)

    column = exchanged(jnp.broadcast_to(table, (Z, ROWS, R)), "z")
    half = exchanged(jnp.broadcast_to(column, (X, Z, ROWS, R)), "x").reshape(HALF, ROWS, R)
    other_half = to_other_core(half)
    terms = evaluated(own, count, half, *tasks)
    terms = terms + evaluated(other, count, other_half, *tasks)
    return exchanged(terms.reshape(8, PTS // 8), "atom").sum(axis=0)


def solution(mesh):
    mesh = Mesh(mesh.devices.reshape(X, Z, CORES, 8), ("x", "z", "core", "atom"))
    shell = ("x", "z", "core")
    in_specs = (
        P(shell),
        P(shell, "atom", None),
        P(shell, "atom"),
        P(shell, "atom", None),
        P(shell, "atom", None),
        P(shell, "atom", None, None),
        P(),
    )
    return jax.shard_map(
        per_device, mesh=mesh, in_specs=in_specs, out_specs=P((*shell, "atom")), check_vma=False
    )
```

```python
import jax
import jax.numpy as jnp
from jax import lax
from jax.experimental import pallas as pl
from jax.experimental.pallas import tpu as pltpu
from jax.sharding import Mesh, PartitionSpec as P

X, Z, CORES = 4, 12, 2
LMAX = 6
LM = 49
ROWS = 56
R = 128
SLOTS = 256
LANES = 128
PTS = 4096
HALF = 48
BLOCK = 24
STEPS = HALF // BLOCK
HIGH, LOW = 32, 128
TILE = 16

f32 = jnp.float32
bf16 = jnp.bfloat16


def radial_grid():
    shape = (R // TILE, TILE, SLOTS)
    grid = lax.broadcasted_iota(jnp.int32, shape, 0) * TILE + lax.broadcasted_iota(jnp.int32, shape, 1)
    return grid.astype(f32).astype(bf16)


def tile_of(row):
    return jnp.broadcast_to(row, (TILE, SLOTS)).astype(bf16)[None]


def hat_rows(grid, index, fraction):
    index = index.astype(f32)
    upper = jnp.where(grid == tile_of(index + 1.0), tile_of(fraction), jnp.zeros((), bf16))
    return jnp.where(grid == tile_of(index), tile_of(1.0 - fraction), upper).reshape(R, SLOTS)


def one_hot_low(grid, points):
    low = tile_of((points & (LOW - 1)).astype(f32))
    return jnp.where(grid == low, jnp.ones((), bf16), jnp.zeros((), bf16)).reshape(LOW, SLOTS)


def is_high(points):
    return lax.broadcasted_iota(jnp.int32, (HIGH, SLOTS), 0) == lax.shift_right_logical(points, 7)


def moments_kernel(
    half_ref,
    count_ref,
    rho_ref,
    point_hbm,
    index_hbm,
    fraction_hbm,
    angular_hbm,
    out_ref,
    point_ref,
    index_ref,
    fraction_ref,
    angular_ref,
    left_ref,
    right_ref,
    task_sems,
    angular_sems,
):
    first = pl.multiple_of(half_ref[0] * HALF, HALF)

    def task_copy(n):
        source = (point_hbm, index_hbm, fraction_hbm)[n]
        target = (point_ref, index_ref, fraction_ref)[n]
        return pltpu.make_async_copy(source.at[pl.ds(first, HALF), :], target, task_sems.at[n])

    def angular_copy(step):
        source = angular_hbm.at[:, pl.ds(first + step * BLOCK, BLOCK), :]
        return pltpu.make_async_copy(source, angular_ref.at[step], angular_sems.at[step])

    for n in range(3):
        task_copy(n).start()
    for step in range(STEPS):
        angular_copy(step).start()

    rho = rho_ref[...]
    big = rho.astype(bf16)
    small = (rho - big.astype(f32)).astype(bf16)
    rho_parts = jnp.concatenate([big, small], axis=1)
    slot = lax.broadcasted_iota(jnp.int32, (1, SLOTS), 1)
    grid = radial_grid()
    filler = jnp.zeros(((ROWS - LM) * BLOCK, LANES), f32)
    left_ref[LM * BLOCK :, :] = filler
    right_ref[LM * BLOCK :, :] = filler
    for n in range(3):
        task_copy(n).wait()

    def block(step, carry):
        base = pl.multiple_of(step * BLOCK, BLOCK)
        points = point_ref[pl.ds(base, BLOCK), :]
        index = index_ref[pl.ds(base, BLOCK), :]
        fraction = fraction_ref[pl.ds(base, BLOCK), :]
        densities = []
        for i in range(BLOCK):
            low = one_hot_low(grid, points[i : i + 1, :])
            columns = jnp.dot(rho_parts, jnp.concatenate([low, low], axis=0), preferred_element_type=f32)
            picked = jnp.sum(jnp.where(is_high(points[i : i + 1, :]), columns, 0.0), axis=0, keepdims=True)
            densities.append(jnp.where(slot < count_ref[first + base + i], picked, 0.0))
        densities = jnp.concatenate(densities, axis=0)
        pltpu.make_async_copy(
            angular_hbm.at[:, pl.ds(first + base, BLOCK), :], angular_ref.at[step], angular_sems.at[step]
        ).wait()
        for m in range(LM):
            weighted = angular_ref[step, m].astype(f32) * densities
            left_ref[m * BLOCK : (m + 1) * BLOCK, :] = weighted[:, :LANES]
            right_ref[m * BLOCK : (m + 1) * BLOCK, :] = weighted[:, LANES:]
        for i in range(BLOCK):
            of_atom = pl.ds(i, ROWS, stride=BLOCK)
            weighted = jnp.concatenate([left_ref[of_atom, :], right_ref[of_atom, :]], axis=1).astype(bf16)
            rows = hat_rows(grid, index[i : i + 1, :], fraction[i : i + 1, :])
            out_ref[base + i] = lax.dot_general(
                weighted, rows, (((1,), (1,)), ((), ())), preferred_element_type=f32
            ).astype(out_ref.dtype)
        return carry

    lax.fori_loop(0, STEPS, block, 0)


def evaluate_kernel(
    half_ref,
    count_ref,
    before_ref,
    table_ref,
    point_ref,
    index_ref,
    fraction_ref,
    angular_ref,
    out_ref,
    left_ref,
    right_ref,
):
    first = pl.multiple_of(half_ref[0] * HALF, HALF)
    slot = lax.broadcasted_iota(jnp.int32, (1, SLOTS), 1)
    grid = radial_grid()

    def block(step, total):
        base = pl.multiple_of(step * BLOCK, BLOCK)
        start = pl.multiple_of(first + base, BLOCK)
        points = point_ref[pl.ds(start, BLOCK), :]
        index = index_ref[pl.ds(start, BLOCK), :]
        fraction = fraction_ref[pl.ds(start, BLOCK), :]
        for i in range(BLOCK):
            rows = hat_rows(grid, index[i : i + 1, :], fraction[i : i + 1, :])
            radial = jnp.dot(table_ref[base + i], rows, preferred_element_type=f32)
            of_atom = pl.ds(i, ROWS, stride=BLOCK)
            left_ref[of_atom, :] = radial[:, :LANES]
            right_ref[of_atom, :] = radial[:, LANES:]
        values = []
        for n, radial_ref in enumerate((left_ref, right_ref)):
            sums = [jnp.zeros((BLOCK, LANES), f32)] * 2
            for m in range(LM):
                angular = angular_ref[m, pl.ds(start, BLOCK), n * LANES : (n + 1) * LANES].astype(f32)
                sums[m % 2] = sums[m % 2] + angular * radial_ref[m * BLOCK : (m + 1) * BLOCK, :]
            values.append(sums[0] + sums[1])
        values = jnp.concatenate(values, axis=1)
        for i in range(BLOCK):
            value = jnp.where(slot < count_ref[start + i], values[i : i + 1, :], 0.0)
            big = value.astype(bf16).astype(f32)
            small = value - big
            high = is_high(points[i : i + 1, :])
            spread = jnp.concatenate([jnp.where(high, big, 0.0), jnp.where(high, small, 0.0)], axis=0)
            low = one_hot_low(grid, points[i : i + 1, :])
            total = total + lax.dot_general(
                spread.astype(bf16), low, (((1,), (1,)), ((), ())), preferred_element_type=f32
            )
        return total

    total = lax.fori_loop(0, STEPS, block, jnp.zeros((2 * HIGH, LOW), f32))
    out_ref[...] = before_ref[...] + (total[:HIGH] + total[HIGH:])


def solve_kernel(parts_ref, green_ref, table_ref):
    moments = jnp.sum(parts_ref[...].astype(f32), axis=0)
    row = lax.broadcasted_iota(jnp.int32, (ROWS, R), 0)
    table = jnp.zeros((ROWS, R), f32)
    for degree in range(LMAX + 1):
        of_degree = (row >= degree * degree) & (row < (degree + 1) * (degree + 1))
        table = table + jnp.dot(
            jnp.where(of_degree, moments, 0.0),
            green_ref[degree],
            precision=lax.Precision.HIGHEST,
            preferred_element_type=f32,
        )
    table_ref[...] = jnp.broadcast_to(table.astype(bf16), (Z, ROWS, R))


VMEM = pl.BlockSpec(memory_space=pltpu.VMEM)
SMEM = pl.BlockSpec(memory_space=pltpu.SMEM)
ANY = pl.BlockSpec(memory_space=pl.ANY)


def moments_of(half, count, rho, points, index, fraction, angular, dtype):
    return pl.pallas_call(
        moments_kernel,
        out_shape=jax.ShapeDtypeStruct((HALF, ROWS, R), dtype),
        in_specs=[SMEM, SMEM, VMEM, ANY, ANY, ANY, ANY],
        out_specs=VMEM,
        scratch_shapes=[
            pltpu.VMEM((HALF, SLOTS), jnp.int32),
            pltpu.VMEM((HALF, SLOTS), jnp.int32),
            pltpu.VMEM((HALF, SLOTS), f32),
            pltpu.VMEM((STEPS, LM, BLOCK, SLOTS), bf16),
            pltpu.VMEM((ROWS * BLOCK, LANES), f32),
            pltpu.VMEM((ROWS * BLOCK, LANES), f32),
            pltpu.SemaphoreType.DMA((3,)),
            pltpu.SemaphoreType.DMA((STEPS,)),
        ],
        name="moments",
    )(half, count, rho, points, index, fraction, angular)


def evaluated(half, count, before, table, points, index, fraction, angular):
    return pl.pallas_call(
        evaluate_kernel,
        out_shape=jax.ShapeDtypeStruct((HIGH, LOW), f32),
        in_specs=[SMEM, SMEM] + [VMEM] * 6,
        out_specs=VMEM,
        scratch_shapes=[pltpu.VMEM((ROWS * BLOCK, LANES), f32)] * 2,
        name="evaluate",
    )(half, count, before, table, points, index, fraction, angular)


def solved(parts, green):
    return pl.pallas_call(
        solve_kernel,
        out_shape=jax.ShapeDtypeStruct((Z, ROWS, R), bf16),
        in_specs=[VMEM, VMEM],
        out_specs=VMEM,
        name="solve",
    )(parts, green)


def exchanged(array, axis):
    return lax.all_to_all(array, axis, split_axis=0, concat_axis=0, tiled=True)


def to_other_core(array):
    return lax.ppermute(array, "core", [(0, 1), (1, 0)])


def near(array):
    return pltpu.with_memory_space_constraint(array, pltpu.VMEM)


def per_device(rho, task_point, task_count, radial_index, fraction, angular, green):
    core = lax.axis_index("core")
    own = core.astype(jnp.int32).reshape(1)
    other = 1 - own
    tasks = (task_point[0], radial_index[0], fraction[0], angular[0].transpose(1, 0, 2))
    count = task_count[0]
    rho = rho.reshape(HIGH, LOW)

    sent = moments_of(other, count, rho, *tasks, bf16)
    arrived = to_other_core(sent)
    kept = moments_of(own, count, rho, *tasks, f32)
    chip = (kept + arrived.astype(f32)).astype(bf16)
    along_x = exchanged(chip.reshape(X, Z, ROWS, R), "x").astype(f32)
    plane = ((along_x[0] + along_x[1]) + (along_x[2] + along_x[3])).astype(bf16)
    column = solved(near(exchanged(plane, "z")), near(green))

    column = exchanged(column, "z")
    half = exchanged(jnp.broadcast_to(column, (X, Z, ROWS, R)), "x").reshape(HALF, ROWS, R)
    other_half = to_other_core(half)
    tasks = [near(array) for array in tasks]
    terms = evaluated(own, count, jnp.zeros((HIGH, LOW), f32), near(half), *tasks)
    terms = evaluated(other, count, terms, near(other_half), *tasks)
    return exchanged(terms.reshape(8, PTS // 8), "atom").sum(axis=0)


def solution(mesh):
    mesh = Mesh(mesh.devices.reshape(X, Z, CORES, 8), ("x", "z", "core", "atom"))
    shell = ("x", "z", "core")
    in_specs = (
        P(shell),
        P(shell, "atom", None),
        P(shell, "atom"),
        P(shell, "atom", None),
        P(shell, "atom", None),
        P(shell, "atom", None, None),
        P(),
    )
    return jax.shard_map(
        per_device, mesh=mesh, in_specs=in_specs, out_specs=P((*shell, "atom")), check_vma=False
    )
```

```python
import jax
import jax.numpy as jnp
from jax import lax
from jax.experimental import pallas as pl
from jax.experimental.pallas import tpu as pltpu
from jax.sharding import Mesh, PartitionSpec as P

X, Z, CORES = 4, 12, 2
LMAX = 6
LM = 49
ROWS = 56
R = 128
SLOTS = 256
LANES = 128
PTS = 4096
HALF = 48
BLOCK = 24
STEPS = HALF // BLOCK
HIGH, LOW = 32, 128
TILE = 16

f32 = jnp.float32
bf16 = jnp.bfloat16


def radial_grid():
    shape = (R // TILE, TILE, SLOTS)
    grid = lax.broadcasted_iota(jnp.int32, shape, 0) * TILE + lax.broadcasted_iota(jnp.int32, shape, 1)
    return grid.astype(f32).astype(bf16)


def tile_of(row):
    return jnp.broadcast_to(row, (TILE, SLOTS)).astype(bf16)[None]


def hat_rows(grid, index, fraction):
    index = index.astype(f32)
    upper = jnp.where(grid == tile_of(index + 1.0), tile_of(fraction), jnp.zeros((), bf16))
    return jnp.where(grid == tile_of(index), tile_of(1.0 - fraction), upper).reshape(R, SLOTS)


def one_hot_low(grid, points):
    low = tile_of((points & (LOW - 1)).astype(f32))
    return jnp.where(grid == low, jnp.ones((), bf16), jnp.zeros((), bf16)).reshape(LOW, SLOTS)


def is_high(points):
    return lax.broadcasted_iota(jnp.int32, (HIGH, SLOTS), 0) == lax.shift_right_logical(points, 7)


def add_moments(base, counts, tasks, angular_rows, rho_ref, out_ref, left_ref, right_ref):
    points, index, fraction = tasks
    rho = rho_ref[...]
    big = rho.astype(bf16)
    small = (rho - big.astype(f32)).astype(bf16)
    rho_parts = jnp.concatenate([big, small], axis=1)
    slot = lax.broadcasted_iota(jnp.int32, (1, SLOTS), 1)
    grid = radial_grid()
    densities = []
    for i in range(BLOCK):
        low = one_hot_low(grid, points[i : i + 1, :])
        columns = jnp.dot(rho_parts, jnp.concatenate([low, low], axis=0), preferred_element_type=f32)
        picked = jnp.sum(jnp.where(is_high(points[i : i + 1, :]), columns, 0.0), axis=0, keepdims=True)
        densities.append(jnp.where(slot < counts(i), picked, 0.0))
    densities = jnp.concatenate(densities, axis=0)
    for m, angular in enumerate(angular_rows()):
        weighted = angular.astype(f32) * densities
        left_ref[m * BLOCK : (m + 1) * BLOCK, :] = weighted[:, :LANES]
        right_ref[m * BLOCK : (m + 1) * BLOCK, :] = weighted[:, LANES:]
    for i in range(BLOCK):
        of_atom = pl.ds(i, ROWS, stride=BLOCK)
        weighted = jnp.concatenate([left_ref[of_atom, :], right_ref[of_atom, :]], axis=1).astype(bf16)
        rows = hat_rows(grid, index[i : i + 1, :], fraction[i : i + 1, :])
        out_ref[base + i] = lax.dot_general(
            weighted, rows, (((1,), (1,)), ((), ())), preferred_element_type=f32
        ).astype(out_ref.dtype)


def fill(left_ref, right_ref):
    filler = jnp.zeros(((ROWS - LM) * BLOCK, LANES), f32)
    left_ref[LM * BLOCK :, :] = filler
    right_ref[LM * BLOCK :, :] = filler


def first_moments_kernel(
    half_ref,
    count_hbm,
    rho_hbm,
    point_hbm,
    index_hbm,
    fraction_hbm,
    angular_hbm,
    out_ref,
    count_ref,
    rho_ref,
    point_ref,
    index_ref,
    fraction_ref,
    angular_ref,
    left_ref,
    right_ref,
    task_sems,
    angular_sems,
):
    first = pl.multiple_of(half_ref[0] * HALF, HALF)
    task_refs = (point_ref, index_ref, fraction_ref)

    def task_copy(n):
        source = (point_hbm, index_hbm, fraction_hbm)[n]
        return pltpu.make_async_copy(source.at[pl.ds(first, HALF), :], task_refs[n], task_sems.at[n])

    def rho_copy():
        return pltpu.make_async_copy(rho_hbm, rho_ref, task_sems.at[3])

    def count_copy():
        return pltpu.make_async_copy(count_hbm, count_ref, task_sems.at[4])

    def angular_copy(step):
        source = angular_hbm.at[:, pl.ds(first + step * BLOCK, BLOCK), :]
        return pltpu.make_async_copy(source, angular_ref.at[step], angular_sems.at[step])

    rho_copy().start()
    count_copy().start()
    for n in range(3):
        task_copy(n).start()
    for step in range(STEPS):
        angular_copy(step).start()
    fill(left_ref, right_ref)
    rho_copy().wait()
    count_copy().wait()
    for n in range(3):
        task_copy(n).wait()

    def block(step, carry):
        base = pl.multiple_of(step * BLOCK, BLOCK)

        def angular_rows():
            angular_copy(step).wait()
            return (angular_ref[step, m] for m in range(LM))

        tasks = [ref[pl.ds(base, BLOCK), :] for ref in task_refs]
        add_moments(
            base, lambda i: count_ref[0, first + base + i], tasks, angular_rows, rho_ref, out_ref, left_ref, right_ref
        )
        return carry

    lax.fori_loop(0, STEPS, block, 0)


def moments_kernel(
    half_ref, count_ref, rho_ref, point_ref, index_ref, fraction_ref, angular_ref, out_ref, left_ref, right_ref
):
    first = pl.multiple_of(half_ref[0] * HALF, HALF)
    fill(left_ref, right_ref)

    def block(step, carry):
        base = pl.multiple_of(step * BLOCK, BLOCK)
        start = pl.multiple_of(first + base, BLOCK)
        tasks = [ref[pl.ds(start, BLOCK), :] for ref in (point_ref, index_ref, fraction_ref)]
        add_moments(
            base,
            lambda i: count_ref[0, start + i],
            tasks,
            lambda: (angular_ref[m, pl.ds(start, BLOCK), :] for m in range(LM)),
            rho_ref,
            out_ref,
            left_ref,
            right_ref,
        )
        return carry

    lax.fori_loop(0, STEPS, block, 0)


def evaluate_kernel(
    half_ref, count_ref, table_ref, point_ref, index_ref, fraction_ref, angular_ref, *refs
):
    *before_ref, out_ref, left_ref, right_ref = refs
    first = pl.multiple_of(half_ref[0] * HALF, HALF)
    slot = lax.broadcasted_iota(jnp.int32, (1, SLOTS), 1)
    grid = radial_grid()

    def block(step, total):
        base = pl.multiple_of(step * BLOCK, BLOCK)
        start = pl.multiple_of(first + base, BLOCK)
        points = point_ref[pl.ds(start, BLOCK), :]
        index = index_ref[pl.ds(start, BLOCK), :]
        fraction = fraction_ref[pl.ds(start, BLOCK), :]
        for i in range(BLOCK):
            rows = hat_rows(grid, index[i : i + 1, :], fraction[i : i + 1, :])
            radial = jnp.dot(table_ref[base + i], rows, preferred_element_type=f32)
            of_atom = pl.ds(i, ROWS, stride=BLOCK)
            left_ref[of_atom, :] = radial[:, :LANES]
            right_ref[of_atom, :] = radial[:, LANES:]
        values = []
        for n, radial_ref in enumerate((left_ref, right_ref)):
            sums = [jnp.zeros((BLOCK, LANES), f32)] * 2
            for m in range(LM):
                angular = angular_ref[m, pl.ds(start, BLOCK), n * LANES : (n + 1) * LANES].astype(f32)
                sums[m % 2] = sums[m % 2] + angular * radial_ref[m * BLOCK : (m + 1) * BLOCK, :]
            values.append(sums[0] + sums[1])
        values = jnp.concatenate(values, axis=1)
        for i in range(BLOCK):
            value = jnp.where(slot < count_ref[0, start + i], values[i : i + 1, :], 0.0)
            big = value.astype(bf16).astype(f32)
            small = value - big
            high = is_high(points[i : i + 1, :])
            spread = jnp.concatenate([jnp.where(high, big, 0.0), jnp.where(high, small, 0.0)], axis=0)
            low = one_hot_low(grid, points[i : i + 1, :])
            total = total + lax.dot_general(
                spread.astype(bf16), low, (((1,), (1,)), ((), ())), preferred_element_type=f32
            )
        return total

    total = lax.fori_loop(0, STEPS, block, jnp.zeros((2 * HIGH, LOW), f32))
    total = total[:HIGH] + total[HIGH:]
    out_ref[...] = total + before_ref[0][...] if before_ref else total


def solve_kernel(parts_ref, green_ref, table_ref):
    moments = jnp.sum(parts_ref[...].astype(f32), axis=0)
    row = lax.broadcasted_iota(jnp.int32, (ROWS, R), 0)
    table = jnp.zeros((ROWS, R), f32)
    for degree in range(LMAX + 1):
        of_degree = (row >= degree * degree) & (row < (degree + 1) * (degree + 1))
        table = table + jnp.dot(
            jnp.where(of_degree, moments, 0.0),
            green_ref[degree],
            precision=lax.Precision.HIGHEST,
            preferred_element_type=f32,
        )
    table_ref[...] = jnp.broadcast_to(table.astype(bf16), (Z, ROWS, R))


VMEM = pl.BlockSpec(memory_space=pltpu.VMEM)
SMEM = pl.BlockSpec(memory_space=pltpu.SMEM)
HBM = pl.BlockSpec(memory_space=pltpu.HBM)
GRANT = pltpu.CompilerParams(vmem_limit_bytes=16 << 20)


def first_moments_of(half, count, rho, points, index, fraction, angular):
    return pl.pallas_call(
        first_moments_kernel,
        out_shape=pltpu.VMEM((HALF, ROWS, R), bf16),
        in_specs=[SMEM] + [HBM] * 6,
        out_specs=VMEM,
        scratch_shapes=[
            pltpu.SMEM((1, 2 * HALF), jnp.int32),
            pltpu.VMEM((HIGH, LOW), f32),
            pltpu.VMEM((HALF, SLOTS), jnp.int32),
            pltpu.VMEM((HALF, SLOTS), jnp.int32),
            pltpu.VMEM((HALF, SLOTS), f32),
            pltpu.VMEM((STEPS, LM, BLOCK, SLOTS), bf16),
            pltpu.VMEM((ROWS * BLOCK, LANES), f32),
            pltpu.VMEM((ROWS * BLOCK, LANES), f32),
            pltpu.SemaphoreType.DMA((5,)),
            pltpu.SemaphoreType.DMA((STEPS,)),
        ],
        compiler_params=GRANT,
        name="first_moments",
    )(half, count, rho, points, index, fraction, angular)


def moments_of(half, count, rho, points, index, fraction, angular):
    return pl.pallas_call(
        moments_kernel,
        out_shape=pltpu.VMEM((HALF, ROWS, R), f32),
        in_specs=[SMEM, SMEM] + [VMEM] * 5,
        out_specs=VMEM,
        scratch_shapes=[pltpu.VMEM((ROWS * BLOCK, LANES), f32)] * 2,
        compiler_params=GRANT,
        name="moments",
    )(half, count, rho, points, index, fraction, angular)


def evaluated(half, count, table, points, index, fraction, angular, *before):
    return pl.pallas_call(
        evaluate_kernel,
        out_shape=pltpu.VMEM((HIGH, LOW), f32),
        in_specs=[SMEM, SMEM] + [VMEM] * (5 + len(before)),
        out_specs=VMEM,
        scratch_shapes=[pltpu.VMEM((ROWS * BLOCK, LANES), f32)] * 2,
        compiler_params=GRANT,
        name="evaluate",
    )(half, count, table, points, index, fraction, angular, *before)


def solved(parts, green):
    return pl.pallas_call(
        solve_kernel,
        out_shape=pltpu.VMEM((Z, ROWS, R), bf16),
        in_specs=[VMEM, VMEM],
        out_specs=VMEM,
        compiler_params=GRANT,
        name="solve",
    )(parts, green)


def exchanged(array, axis):
    return lax.all_to_all(array, axis, split_axis=0, concat_axis=0, tiled=True)


def to_other_core(array):
    return lax.ppermute(array, "core", [(0, 1), (1, 0)])


def far(array):
    return pltpu.with_memory_space_constraint(array, pltpu.HBM)


def near(array):
    return pltpu.with_memory_space_constraint(array, pltpu.VMEM)


def per_device(rho, task_point, task_count, radial_index, fraction, angular, green):
    core = lax.axis_index("core")
    own = core.astype(jnp.int32).reshape(1)
    other = 1 - own
    tasks = (task_point[0], radial_index[0], fraction[0], angular[0].transpose(1, 0, 2))
    count = task_count
    rho = rho.reshape(HIGH, LOW)

    sent = first_moments_of(other, *(far(array) for array in (count, rho, *tasks)))
    arrived = to_other_core(sent)
    tasks = [near(array) for array in tasks]
    kept = moments_of(own, count, near(rho), *tasks)
    chip = (kept + arrived.astype(f32)).astype(bf16)
    along_x = exchanged(chip.reshape(X, Z, ROWS, R), "x").astype(f32)
    plane = ((along_x[0] + along_x[1]) + (along_x[2] + along_x[3])).astype(bf16)
    column = solved(near(exchanged(plane, "z")), near(green))

    column = exchanged(column, "z")
    half = exchanged(jnp.broadcast_to(column, (X, Z, ROWS, R)), "x").reshape(HALF, ROWS, R)
    other_half = to_other_core(half)
    terms = evaluated(own, count, near(half), *tasks)
    terms = evaluated(other, count, near(other_half), *tasks, terms)
    return exchanged(terms.reshape(8, PTS // 8), "atom").sum(axis=0)


def solution(mesh):
    mesh = Mesh(mesh.devices.reshape(X, Z, CORES, 8), ("x", "z", "core", "atom"))
    shell = ("x", "z", "core")
    in_specs = (
        P(shell),
        P(shell, "atom", None),
        P(shell, "atom"),
        P(shell, "atom", None),
        P(shell, "atom", None),
        P(shell, "atom", None, None),
        P(),
    )
    return jax.shard_map(
        per_device, mesh=mesh, in_specs=in_specs, out_specs=P((*shell, "atom")), check_vma=False
    )
```

```python
import jax
import jax.numpy as jnp
from jax import lax
from jax.experimental import pallas as pl
from jax.experimental.pallas import tpu as pltpu
from jax.sharding import Mesh, PartitionSpec as P

X, Z, CORES = 4, 12, 2
LMAX = 6
LM = 49
ROWS = 56
R = 128
SLOTS = 256
LANES = 128
PTS = 4096
HALF = X * Z
BLOCK = 24
STEPS = HALF // BLOCK
HIGH, LOW = 32, 128
TILE = 16

f32 = jnp.float32
bf16 = jnp.bfloat16


def radial_grid():
    shape = (R // TILE, TILE, SLOTS)
    grid = lax.broadcasted_iota(jnp.int32, shape, 0) * TILE + lax.broadcasted_iota(jnp.int32, shape, 1)
    return grid.astype(f32).astype(bf16)


def tile_of(row):
    return jnp.broadcast_to(row, (TILE, SLOTS)).astype(bf16)[None]


def hat_rows(grid, index, fraction):
    index = index.astype(f32)
    upper = jnp.where(grid == tile_of(index + 1.0), tile_of(fraction), jnp.zeros((), bf16))
    return jnp.where(grid == tile_of(index), tile_of(1.0 - fraction), upper).reshape(R, SLOTS)


def one_hot_low(grid, points):
    low = tile_of((points & (LOW - 1)).astype(f32))
    return jnp.where(grid == low, jnp.ones((), bf16), jnp.zeros((), bf16)).reshape(LOW, SLOTS)


def is_high(points):
    return lax.broadcasted_iota(jnp.int32, (HIGH, SLOTS), 0) == lax.shift_right_logical(points, 7)


def add_moments(base, counts, tasks, angular_rows, rho_ref, out_ref, left_ref, right_ref):
    points, index, fraction = tasks
    rho = rho_ref[...]
    big = rho.astype(bf16)
    small = (rho - big.astype(f32)).astype(bf16)
    rho_parts = jnp.concatenate([big, small], axis=1)
    slot = lax.broadcasted_iota(jnp.int32, (1, SLOTS), 1)
    grid = radial_grid()
    densities = []
    for i in range(BLOCK):
        low = one_hot_low(grid, points[i : i + 1, :])
        columns = jnp.dot(rho_parts, jnp.concatenate([low, low], axis=0), preferred_element_type=f32)
        picked = jnp.sum(jnp.where(is_high(points[i : i + 1, :]), columns, 0.0), axis=0, keepdims=True)
        densities.append(jnp.where(slot < counts(i), picked, 0.0))
    densities = jnp.concatenate(densities, axis=0)
    for m, angular in enumerate(angular_rows()):
        weighted = angular.astype(f32) * densities
        left_ref[m * BLOCK : (m + 1) * BLOCK, :] = weighted[:, :LANES]
        right_ref[m * BLOCK : (m + 1) * BLOCK, :] = weighted[:, LANES:]
    for i in range(BLOCK):
        of_atom = pl.ds(i, ROWS, stride=BLOCK)
        weighted = jnp.concatenate([left_ref[of_atom, :], right_ref[of_atom, :]], axis=1).astype(bf16)
        rows = hat_rows(grid, index[i : i + 1, :], fraction[i : i + 1, :])
        out_ref[base + i] = lax.dot_general(
            weighted, rows, (((1,), (1,)), ((), ())), preferred_element_type=f32
        ).astype(out_ref.dtype)


def fill(left_ref, right_ref):
    filler = jnp.zeros(((ROWS - LM) * BLOCK, LANES), f32)
    left_ref[LM * BLOCK :, :] = filler
    right_ref[LM * BLOCK :, :] = filler


def first_moments_kernel(
    half_ref,
    count_hbm,
    rho_hbm,
    point_hbm,
    index_hbm,
    fraction_hbm,
    angular_hbm,
    out_ref,
    count_ref,
    rho_ref,
    point_ref,
    index_ref,
    fraction_ref,
    angular_ref,
    left_ref,
    right_ref,
    task_sems,
    angular_sems,
):
    first = pl.multiple_of(half_ref[0] * HALF, HALF)
    task_refs = (point_ref, index_ref, fraction_ref)

    def task_copy(n):
        source = (point_hbm, index_hbm, fraction_hbm)[n]
        return pltpu.make_async_copy(source.at[pl.ds(first, HALF), :], task_refs[n], task_sems.at[n])

    def rho_copy():
        return pltpu.make_async_copy(rho_hbm, rho_ref, task_sems.at[3])

    def count_copy():
        return pltpu.make_async_copy(count_hbm, count_ref, task_sems.at[4])

    def angular_copy(step):
        source = angular_hbm.at[:, pl.ds(first + step * BLOCK, BLOCK), :]
        return pltpu.make_async_copy(source, angular_ref.at[step], angular_sems.at[step])

    rho_copy().start()
    count_copy().start()
    for n in range(3):
        task_copy(n).start()
    for step in range(STEPS):
        angular_copy(step).start()
    fill(left_ref, right_ref)
    rho_copy().wait()
    count_copy().wait()
    for n in range(3):
        task_copy(n).wait()

    def block(step, carry):
        base = pl.multiple_of(step * BLOCK, BLOCK)

        def angular_rows():
            angular_copy(step).wait()
            return (angular_ref[step, m] for m in range(LM))

        tasks = [ref[pl.ds(base, BLOCK), :] for ref in task_refs]
        add_moments(
            base, lambda i: count_ref[0, first + base + i], tasks, angular_rows, rho_ref, out_ref, left_ref, right_ref
        )
        return carry

    lax.fori_loop(0, STEPS, block, 0)


def moments_kernel(
    half_ref, count_ref, rho_ref, point_ref, index_ref, fraction_ref, angular_ref, out_ref, left_ref, right_ref
):
    first = pl.multiple_of(half_ref[0] * HALF, HALF)
    fill(left_ref, right_ref)

    def block(step, carry):
        base = pl.multiple_of(step * BLOCK, BLOCK)
        start = pl.multiple_of(first + base, BLOCK)
        tasks = [ref[pl.ds(start, BLOCK), :] for ref in (point_ref, index_ref, fraction_ref)]
        add_moments(
            base,
            lambda i: count_ref[0, start + i],
            tasks,
            lambda: (angular_ref[m, pl.ds(start, BLOCK), :] for m in range(LM)),
            rho_ref,
            out_ref,
            left_ref,
            right_ref,
        )
        return carry

    lax.fori_loop(0, STEPS, block, 0)


def evaluate_kernel(
    half_ref, count_ref, table_ref, point_ref, index_ref, fraction_ref, angular_ref, *refs
):
    *before_ref, out_ref, left_ref, right_ref = refs
    first = pl.multiple_of(half_ref[0] * HALF, HALF)
    slot = lax.broadcasted_iota(jnp.int32, (1, SLOTS), 1)
    grid = radial_grid()

    def block(step, total):
        base = pl.multiple_of(step * BLOCK, BLOCK)
        start = pl.multiple_of(first + base, BLOCK)
        points = point_ref[pl.ds(start, BLOCK), :]
        index = index_ref[pl.ds(start, BLOCK), :]
        fraction = fraction_ref[pl.ds(start, BLOCK), :]
        for i in range(BLOCK):
            rows = hat_rows(grid, index[i : i + 1, :], fraction[i : i + 1, :])
            radial = jnp.dot(table_ref[base + i], rows, preferred_element_type=f32)
            of_atom = pl.ds(i, ROWS, stride=BLOCK)
            left_ref[of_atom, :] = radial[:, :LANES]
            right_ref[of_atom, :] = radial[:, LANES:]
        values = []
        for n, radial_ref in enumerate((left_ref, right_ref)):
            sums = [jnp.zeros((BLOCK, LANES), f32)] * 2
            for m in range(LM):
                angular = angular_ref[m, pl.ds(start, BLOCK), n * LANES : (n + 1) * LANES].astype(f32)
                sums[m % 2] = sums[m % 2] + angular * radial_ref[m * BLOCK : (m + 1) * BLOCK, :]
            values.append(sums[0] + sums[1])
        values = jnp.concatenate(values, axis=1)
        for i in range(BLOCK):
            value = jnp.where(slot < count_ref[0, start + i], values[i : i + 1, :], 0.0)
            big = value.astype(bf16).astype(f32)
            small = value - big
            high = is_high(points[i : i + 1, :])
            spread = jnp.concatenate([jnp.where(high, big, 0.0), jnp.where(high, small, 0.0)], axis=0)
            low = one_hot_low(grid, points[i : i + 1, :])
            total = total + lax.dot_general(
                spread.astype(bf16), low, (((1,), (1,)), ((), ())), preferred_element_type=f32
            )
        return total

    total = lax.fori_loop(0, STEPS, block, jnp.zeros((2 * HIGH, LOW), f32))
    total = total[:HIGH] + total[HIGH:]
    out_ref[...] = total + before_ref[0][...] if before_ref else total


def solve_kernel(parts_ref, green_ref, table_ref):
    moments = jnp.sum(parts_ref[...].astype(f32), axis=0)
    row = lax.broadcasted_iota(jnp.int32, (ROWS, R), 0)
    table = jnp.zeros((ROWS, R), f32)
    for degree in range(LMAX + 1):
        of_degree = (row >= degree * degree) & (row < (degree + 1) * (degree + 1))
        table = table + jnp.dot(
            jnp.where(of_degree, moments, 0.0),
            green_ref[degree],
            precision=lax.Precision.HIGHEST,
            preferred_element_type=f32,
        )
    table_ref[...] = jnp.broadcast_to(table.astype(bf16), (HALF, ROWS, R))


VMEM = pl.BlockSpec(memory_space=pltpu.VMEM)
SMEM = pl.BlockSpec(memory_space=pltpu.SMEM)
HBM = pl.BlockSpec(memory_space=pltpu.HBM)
GRANT = pltpu.CompilerParams(vmem_limit_bytes=16 << 20)


def first_moments_of(half, count, rho, points, index, fraction, angular):
    return pl.pallas_call(
        first_moments_kernel,
        out_shape=pltpu.VMEM((HALF, ROWS, R), bf16),
        in_specs=[SMEM] + [HBM] * 6,
        out_specs=VMEM,
        scratch_shapes=[
            pltpu.SMEM((1, 2 * HALF), jnp.int32),
            pltpu.VMEM((HIGH, LOW), f32),
            pltpu.VMEM((HALF, SLOTS), jnp.int32),
            pltpu.VMEM((HALF, SLOTS), jnp.int32),
            pltpu.VMEM((HALF, SLOTS), f32),
            pltpu.VMEM((STEPS, LM, BLOCK, SLOTS), bf16),
            pltpu.VMEM((ROWS * BLOCK, LANES), f32),
            pltpu.VMEM((ROWS * BLOCK, LANES), f32),
            pltpu.SemaphoreType.DMA((5,)),
            pltpu.SemaphoreType.DMA((STEPS,)),
        ],
        compiler_params=GRANT,
        name="first_moments",
    )(half, count, rho, points, index, fraction, angular)


def moments_of(half, count, rho, points, index, fraction, angular):
    return pl.pallas_call(
        moments_kernel,
        out_shape=pltpu.VMEM((HALF, ROWS, R), f32),
        in_specs=[SMEM, SMEM] + [VMEM] * 5,
        out_specs=VMEM,
        scratch_shapes=[pltpu.VMEM((ROWS * BLOCK, LANES), f32)] * 2,
        compiler_params=GRANT,
        name="moments",
    )(half, count, rho, points, index, fraction, angular)


def evaluated(half, count, table, points, index, fraction, angular, *before):
    return pl.pallas_call(
        evaluate_kernel,
        out_shape=pltpu.VMEM((HIGH, LOW), f32),
        in_specs=[SMEM, SMEM] + [VMEM] * (5 + len(before)),
        out_specs=VMEM,
        scratch_shapes=[pltpu.VMEM((ROWS * BLOCK, LANES), f32)] * 2,
        compiler_params=GRANT,
        name="evaluate",
    )(half, count, table, points, index, fraction, angular, *before)


def solved(parts, green):
    return pl.pallas_call(
        solve_kernel,
        out_shape=pltpu.VMEM((HALF, ROWS, R), bf16),
        in_specs=[VMEM, VMEM],
        out_specs=VMEM,
        compiler_params=GRANT,
        name="solve",
    )(parts, green)


def exchanged(array, axis):
    return lax.all_to_all(array, axis, split_axis=0, concat_axis=0, tiled=True)


def to_other_core(array):
    return lax.ppermute(array, "core", [(0, 1), (1, 0)])


def far(array):
    return pltpu.with_memory_space_constraint(array, pltpu.HBM)


def near(array):
    return pltpu.with_memory_space_constraint(array, pltpu.VMEM)


def per_device(rho, task_point, task_count, radial_index, fraction, angular, green):
    core = lax.axis_index("core")
    own = core.astype(jnp.int32).reshape(1)
    other = 1 - own
    tasks = (task_point[0], radial_index[0], fraction[0], angular[0].transpose(1, 0, 2))
    count = task_count
    rho = rho.reshape(HIGH, LOW)

    sent = first_moments_of(other, *(far(array) for array in (count, rho, *tasks)))
    arrived = to_other_core(sent)
    tasks = [near(array) for array in tasks]
    kept = moments_of(own, count, near(rho), *tasks)
    chip = (kept + arrived.astype(f32)).astype(bf16)
    parts = exchanged(chip, ("x", "z"))
    half = exchanged(solved(near(parts), near(green)), ("x", "z"))
    other_half = to_other_core(half)
    terms = evaluated(own, count, near(half), *tasks)
    terms = evaluated(other, count, near(other_half), *tasks, terms)
    return exchanged(terms.reshape(8, PTS // 8), "atom").sum(axis=0)


def solution(mesh):
    mesh = Mesh(mesh.devices.reshape(X, Z, CORES, 8), ("x", "z", "core", "atom"))
    shell = ("x", "z", "core")
    in_specs = (
        P(shell),
        P(shell, "atom", None),
        P(shell, "atom"),
        P(shell, "atom", None),
        P(shell, "atom", None),
        P(shell, "atom", None, None),
        P(),
    )
    return jax.shard_map(
        per_device, mesh=mesh, in_specs=in_specs, out_specs=P((*shell, "atom")), check_vma=False
    )
```

```python
import jax
import jax.numpy as jnp
from jax import lax
from jax.experimental import pallas as pl
from jax.experimental.pallas import tpu as pltpu
from jax.sharding import Mesh, PartitionSpec as P

X, BLOCKS, PARTS, CORES = 4, 4, 3, 2
IN_BLOCK = X * PARTS
LMAX = 6
LM = 49
ROWS = 56
R = 128
SLOTS = 256
LANES = 128
PTS = 4096
HALF = IN_BLOCK * BLOCKS
BLOCK = 24
STEPS = HALF // BLOCK
HIGH, LOW = 32, 128
TILE = 16

f32 = jnp.float32
bf16 = jnp.bfloat16


def radial_grid():
    shape = (R // TILE, TILE, SLOTS)
    grid = lax.broadcasted_iota(jnp.int32, shape, 0) * TILE + lax.broadcasted_iota(jnp.int32, shape, 1)
    return grid.astype(f32).astype(bf16)


def tile_of(row):
    return jnp.broadcast_to(row, (TILE, SLOTS)).astype(bf16)[None]


def hat_rows(grid, index, fraction):
    index = index.astype(f32)
    upper = jnp.where(grid == tile_of(index + 1.0), tile_of(fraction), jnp.zeros((), bf16))
    return jnp.where(grid == tile_of(index), tile_of(1.0 - fraction), upper).reshape(R, SLOTS)


def one_hot_low(grid, points):
    low = tile_of((points & (LOW - 1)).astype(f32))
    return jnp.where(grid == low, jnp.ones((), bf16), jnp.zeros((), bf16)).reshape(LOW, SLOTS)


def is_high(points):
    return lax.broadcasted_iota(jnp.int32, (HIGH, SLOTS), 0) == lax.shift_right_logical(points, 7)


def add_moments(base, counts, tasks, angular_rows, rho_ref, out_ref, left_ref, right_ref):
    points, index, fraction = tasks
    rho = rho_ref[...]
    big = rho.astype(bf16)
    small = (rho - big.astype(f32)).astype(bf16)
    rho_parts = jnp.concatenate([big, small], axis=1)
    slot = lax.broadcasted_iota(jnp.int32, (1, SLOTS), 1)
    grid = radial_grid()
    densities = []
    for i in range(BLOCK):
        low = one_hot_low(grid, points[i : i + 1, :])
        columns = jnp.dot(rho_parts, jnp.concatenate([low, low], axis=0), preferred_element_type=f32)
        picked = jnp.sum(jnp.where(is_high(points[i : i + 1, :]), columns, 0.0), axis=0, keepdims=True)
        densities.append(jnp.where(slot < counts(i), picked, 0.0))
    densities = jnp.concatenate(densities, axis=0)
    for m, angular in enumerate(angular_rows()):
        weighted = angular.astype(f32) * densities
        left_ref[m * BLOCK : (m + 1) * BLOCK, :] = weighted[:, :LANES]
        right_ref[m * BLOCK : (m + 1) * BLOCK, :] = weighted[:, LANES:]
    for i in range(BLOCK):
        of_atom = pl.ds(i, ROWS, stride=BLOCK)
        weighted = jnp.concatenate([left_ref[of_atom, :], right_ref[of_atom, :]], axis=1).astype(bf16)
        rows = hat_rows(grid, index[i : i + 1, :], fraction[i : i + 1, :])
        out_ref[base + i] = lax.dot_general(
            weighted, rows, (((1,), (1,)), ((), ())), preferred_element_type=f32
        ).astype(out_ref.dtype)


def fill(left_ref, right_ref):
    filler = jnp.zeros(((ROWS - LM) * BLOCK, LANES), f32)
    left_ref[LM * BLOCK :, :] = filler
    right_ref[LM * BLOCK :, :] = filler


def first_moments_kernel(
    half_ref,
    count_hbm,
    rho_hbm,
    point_hbm,
    index_hbm,
    fraction_hbm,
    angular_hbm,
    out_ref,
    count_ref,
    rho_ref,
    point_ref,
    index_ref,
    fraction_ref,
    angular_ref,
    left_ref,
    right_ref,
    task_sems,
    angular_sems,
):
    first = pl.multiple_of(half_ref[0] * HALF, HALF)
    task_refs = (point_ref, index_ref, fraction_ref)

    def task_copy(n):
        source = (point_hbm, index_hbm, fraction_hbm)[n]
        return pltpu.make_async_copy(source.at[pl.ds(first, HALF), :], task_refs[n], task_sems.at[n])

    def rho_copy():
        return pltpu.make_async_copy(rho_hbm, rho_ref, task_sems.at[3])

    def count_copy():
        return pltpu.make_async_copy(count_hbm, count_ref, task_sems.at[4])

    def angular_copy(step):
        source = angular_hbm.at[:, pl.ds(first + step * BLOCK, BLOCK), :]
        return pltpu.make_async_copy(source, angular_ref.at[step], angular_sems.at[step])

    rho_copy().start()
    count_copy().start()
    for n in range(3):
        task_copy(n).start()
    for step in range(STEPS):
        angular_copy(step).start()
    fill(left_ref, right_ref)
    rho_copy().wait()
    count_copy().wait()
    for n in range(3):
        task_copy(n).wait()

    def block(step, carry):
        base = pl.multiple_of(step * BLOCK, BLOCK)

        def angular_rows():
            angular_copy(step).wait()
            return (angular_ref[step, m] for m in range(LM))

        tasks = [ref[pl.ds(base, BLOCK), :] for ref in task_refs]
        add_moments(
            base, lambda i: count_ref[0, first + base + i], tasks, angular_rows, rho_ref, out_ref, left_ref, right_ref
        )
        return carry

    lax.fori_loop(0, STEPS, block, 0)


def moments_kernel(
    half_ref, count_ref, rho_ref, point_ref, index_ref, fraction_ref, angular_ref, out_ref, left_ref, right_ref
):
    first = pl.multiple_of(half_ref[0] * HALF, HALF)
    fill(left_ref, right_ref)

    def block(step, carry):
        base = pl.multiple_of(step * BLOCK, BLOCK)
        start = pl.multiple_of(first + base, BLOCK)
        tasks = [ref[pl.ds(start, BLOCK), :] for ref in (point_ref, index_ref, fraction_ref)]
        add_moments(
            base,
            lambda i: count_ref[0, start + i],
            tasks,
            lambda: (angular_ref[m, pl.ds(start, BLOCK), :] for m in range(LM)),
            rho_ref,
            out_ref,
            left_ref,
            right_ref,
        )
        return carry

    lax.fori_loop(0, STEPS, block, 0)


def evaluate_kernel(
    half_ref, count_ref, table_ref, point_ref, index_ref, fraction_ref, angular_ref, *refs
):
    *before_ref, out_ref, left_ref, right_ref = refs
    first = pl.multiple_of(half_ref[0] * HALF, HALF)
    slot = lax.broadcasted_iota(jnp.int32, (1, SLOTS), 1)
    grid = radial_grid()

    def block(step, total):
        base = pl.multiple_of(step * BLOCK, BLOCK)
        start = pl.multiple_of(first + base, BLOCK)
        points = point_ref[pl.ds(start, BLOCK), :]
        index = index_ref[pl.ds(start, BLOCK), :]
        fraction = fraction_ref[pl.ds(start, BLOCK), :]
        for i in range(BLOCK):
            rows = hat_rows(grid, index[i : i + 1, :], fraction[i : i + 1, :])
            radial = jnp.dot(table_ref[base + i], rows, preferred_element_type=f32)
            of_atom = pl.ds(i, ROWS, stride=BLOCK)
            left_ref[of_atom, :] = radial[:, :LANES]
            right_ref[of_atom, :] = radial[:, LANES:]
        values = []
        for n, radial_ref in enumerate((left_ref, right_ref)):
            sums = [jnp.zeros((BLOCK, LANES), f32)] * 2
            for m in range(LM):
                angular = angular_ref[m, pl.ds(start, BLOCK), n * LANES : (n + 1) * LANES].astype(f32)
                sums[m % 2] = sums[m % 2] + angular * radial_ref[m * BLOCK : (m + 1) * BLOCK, :]
            values.append(sums[0] + sums[1])
        values = jnp.concatenate(values, axis=1)
        for i in range(BLOCK):
            value = jnp.where(slot < count_ref[0, start + i], values[i : i + 1, :], 0.0)
            big = value.astype(bf16).astype(f32)
            small = value - big
            high = is_high(points[i : i + 1, :])
            spread = jnp.concatenate([jnp.where(high, big, 0.0), jnp.where(high, small, 0.0)], axis=0)
            low = one_hot_low(grid, points[i : i + 1, :])
            total = total + lax.dot_general(
                spread.astype(bf16), low, (((1,), (1,)), ((), ())), preferred_element_type=f32
            )
        return total

    total = lax.fori_loop(0, STEPS, block, jnp.zeros((2 * HIGH, LOW), f32))
    total = total[:HIGH] + total[HIGH:]
    out_ref[...] = total + before_ref[0][...] if before_ref else total


def sum_kernel(arrived_ref, out_ref):
    for n in range(BLOCKS):
        plane = jnp.sum(arrived_ref[:, n].astype(f32), axis=0).astype(bf16)
        out_ref[:, n] = jnp.broadcast_to(plane, (BLOCKS, ROWS, R))


def solve_kernel(parts_ref, green_ref, table_ref):
    moments = jnp.sum(parts_ref[...].astype(f32), axis=0)
    tiles = [jnp.zeros((BLOCKS, 8, R), f32)] * (ROWS // 8)
    for degree in range(LMAX + 1):
        start, stop = degree * degree, (degree + 1) * (degree + 1)
        first, last = start // 8, (stop - 1) // 8 + 1
        count = (last - first) * 8
        row = lax.broadcasted_iota(jnp.int32, (BLOCKS, count, R), 1) + first * 8
        of_degree = jnp.where((row >= start) & (row < stop), moments[:, first * 8 : last * 8], 0.0)
        solved = jnp.dot(
            of_degree.reshape(BLOCKS * count, R),
            green_ref[degree],
            precision=lax.Precision.HIGHEST,
            preferred_element_type=f32,
        ).reshape(BLOCKS, count, R)
        for tile in range(first, last):
            tiles[tile] = tiles[tile] + solved[:, (tile - first) * 8 : (tile - first + 1) * 8]
    table = jnp.concatenate(tiles, axis=1).astype(bf16)
    table_ref[...] = jnp.broadcast_to(table, (IN_BLOCK, BLOCKS, ROWS, R))


VMEM = pl.BlockSpec(memory_space=pltpu.VMEM)
SMEM = pl.BlockSpec(memory_space=pltpu.SMEM)
HBM = pl.BlockSpec(memory_space=pltpu.HBM)
GRANT = pltpu.CompilerParams(vmem_limit_bytes=16 << 20)


def first_moments_of(half, count, rho, points, index, fraction, angular):
    return pl.pallas_call(
        first_moments_kernel,
        out_shape=pltpu.VMEM((HALF, ROWS, R), bf16),
        in_specs=[SMEM] + [HBM] * 6,
        out_specs=VMEM,
        scratch_shapes=[
            pltpu.SMEM((1, 2 * HALF), jnp.int32),
            pltpu.VMEM((HIGH, LOW), f32),
            pltpu.VMEM((HALF, SLOTS), jnp.int32),
            pltpu.VMEM((HALF, SLOTS), jnp.int32),
            pltpu.VMEM((HALF, SLOTS), f32),
            pltpu.VMEM((STEPS, LM, BLOCK, SLOTS), bf16),
            pltpu.VMEM((ROWS * BLOCK, LANES), f32),
            pltpu.VMEM((ROWS * BLOCK, LANES), f32),
            pltpu.SemaphoreType.DMA((5,)),
            pltpu.SemaphoreType.DMA((STEPS,)),
        ],
        compiler_params=GRANT,
        name="first_moments",
    )(half, count, rho, points, index, fraction, angular)


def moments_of(half, count, rho, points, index, fraction, angular):
    return pl.pallas_call(
        moments_kernel,
        out_shape=pltpu.VMEM((HALF, ROWS, R), f32),
        in_specs=[SMEM, SMEM] + [VMEM] * 5,
        out_specs=VMEM,
        scratch_shapes=[pltpu.VMEM((ROWS * BLOCK, LANES), f32)] * 2,
        compiler_params=GRANT,
        name="moments",
    )(half, count, rho, points, index, fraction, angular)


def evaluated(half, count, table, points, index, fraction, angular, *before):
    return pl.pallas_call(
        evaluate_kernel,
        out_shape=pltpu.VMEM((HIGH, LOW), f32),
        in_specs=[SMEM, SMEM] + [VMEM] * (5 + len(before)),
        out_specs=VMEM,
        scratch_shapes=[pltpu.VMEM((ROWS * BLOCK, LANES), f32)] * 2,
        compiler_params=GRANT,
        name="evaluate",
    )(half, count, table, points, index, fraction, angular, *before)


def summed(arrived):
    return pl.pallas_call(
        sum_kernel,
        out_shape=pltpu.VMEM((BLOCKS, BLOCKS, ROWS, R), bf16),
        in_specs=[VMEM],
        out_specs=VMEM,
        compiler_params=GRANT,
        name="sum",
    )(arrived)


def solved(parts, green):
    return pl.pallas_call(
        solve_kernel,
        out_shape=pltpu.VMEM((IN_BLOCK, BLOCKS, ROWS, R), bf16),
        in_specs=[VMEM, VMEM],
        out_specs=VMEM,
        compiler_params=GRANT,
        name="solve",
    )(parts, green)


def exchanged(array, axis):
    return lax.all_to_all(array, axis, split_axis=0, concat_axis=0, tiled=True)


def to_other_core(array):
    return lax.ppermute(array, "core", [(0, 1), (1, 0)])


def far(array):
    return pltpu.with_memory_space_constraint(array, pltpu.HBM)


def near(array):
    return pltpu.with_memory_space_constraint(array, pltpu.VMEM)


def per_device(rho, task_point, task_count, radial_index, fraction, angular, green):
    core = lax.axis_index("core")
    own = core.astype(jnp.int32).reshape(1)
    other = 1 - own
    tasks = (task_point[0], radial_index[0], fraction[0], angular[0].transpose(1, 0, 2))
    count = task_count
    rho = rho.reshape(HIGH, LOW)

    sent = first_moments_of(other, *(far(array) for array in (count, rho, *tasks)))
    arrived = to_other_core(sent)
    tasks = [near(array) for array in tasks]
    kept = moments_of(own, count, near(rho), *tasks)
    chip = (kept + arrived.astype(f32)).astype(bf16)
    arrived = exchanged(chip.reshape(IN_BLOCK, BLOCKS, ROWS, R), ("x", "part"))
    parts = exchanged(summed(near(arrived)), "block")
    half = exchanged(solved(near(parts), near(green)), ("x", "part")).reshape(HALF, ROWS, R)
    other_half = to_other_core(half)
    terms = evaluated(own, count, near(half), *tasks)
    terms = evaluated(other, count, near(other_half), *tasks, terms)
    return exchanged(terms.reshape(8, PTS // 8), "atom").sum(axis=0)


def solution(mesh):
    mesh = Mesh(mesh.devices.reshape(X, BLOCKS, PARTS, CORES, 8), ("x", "block", "part", "core", "atom"))
    shell = ("x", "block", "part", "core")
    in_specs = (
        P(shell),
        P(shell, "atom", None),
        P(shell, "atom"),
        P(shell, "atom", None),
        P(shell, "atom", None),
        P(shell, "atom", None, None),
        P(),
    )
    return jax.shard_map(
        per_device, mesh=mesh, in_specs=in_specs, out_specs=P((*shell, "atom")), check_vma=False
    )
```

```python
import jax
import jax.numpy as jnp
from jax import lax
from jax.experimental import pallas as pl
from jax.experimental.pallas import tpu as pltpu
from jax.sharding import Mesh, PartitionSpec as P

X, BLOCKS, PARTS, CORES = 4, 4, 3, 2
IN_BLOCK = X * PARTS
LMAX = 6
LM = 49
ROWS = 56
R = 128
SLOTS = 256
LANES = 128
PTS = 4096
HALF = IN_BLOCK * BLOCKS
BLOCK = 24
STEPS = HALF // BLOCK
HIGH, LOW = 32, 128
TILE = 16

f32 = jnp.float32
bf16 = jnp.bfloat16


def radial_grid():
    shape = (R // TILE, TILE, SLOTS)
    grid = lax.broadcasted_iota(jnp.int32, shape, 0) * TILE + lax.broadcasted_iota(jnp.int32, shape, 1)
    return grid.astype(f32).astype(bf16)


def tile_of(row):
    return jnp.broadcast_to(row, (TILE, SLOTS)).astype(bf16)[None]


def hat_rows(grid, index, fraction):
    index = index.astype(f32)
    upper = jnp.where(grid == tile_of(index + 1.0), tile_of(fraction), jnp.zeros((), bf16))
    return jnp.where(grid == tile_of(index), tile_of(1.0 - fraction), upper).reshape(R, SLOTS)


def one_hot_low(grid, points):
    low = tile_of((points & (LOW - 1)).astype(f32))
    return jnp.where(grid == low, jnp.ones((), bf16), jnp.zeros((), bf16)).reshape(LOW, SLOTS)


def is_high(points):
    return lax.broadcasted_iota(jnp.int32, (HIGH, SLOTS), 0) == lax.shift_right_logical(points, 7)


def add_moments(base, counts, tasks, angular_rows, rho_ref, out_ref, left_ref, right_ref):
    points, index, fraction = tasks
    rho = rho_ref[...]
    big = rho.astype(bf16)
    small = (rho - big.astype(f32)).astype(bf16)
    rho_parts = jnp.concatenate([big, small], axis=1)
    slot = lax.broadcasted_iota(jnp.int32, (1, SLOTS), 1)
    grid = radial_grid()
    densities = []
    for i in range(BLOCK):
        low = one_hot_low(grid, points[i : i + 1, :])
        columns = jnp.dot(rho_parts, jnp.concatenate([low, low], axis=0), preferred_element_type=f32)
        picked = jnp.sum(jnp.where(is_high(points[i : i + 1, :]), columns, 0.0), axis=0, keepdims=True)
        densities.append(jnp.where(slot < counts(i), picked, 0.0))
    densities = jnp.concatenate(densities, axis=0)
    for m, angular in enumerate(angular_rows()):
        weighted = angular.astype(f32) * densities
        left_ref[m * BLOCK : (m + 1) * BLOCK, :] = weighted[:, :LANES]
        right_ref[m * BLOCK : (m + 1) * BLOCK, :] = weighted[:, LANES:]
    for i in range(BLOCK):
        of_atom = pl.ds(i, ROWS, stride=BLOCK)
        weighted = jnp.concatenate([left_ref[of_atom, :], right_ref[of_atom, :]], axis=1).astype(bf16)
        rows = hat_rows(grid, index[i : i + 1, :], fraction[i : i + 1, :])
        out_ref[base + i] = lax.dot_general(
            weighted, rows, (((1,), (1,)), ((), ())), preferred_element_type=f32
        ).astype(out_ref.dtype)


def fill(left_ref, right_ref):
    filler = jnp.zeros(((ROWS - LM) * BLOCK, LANES), f32)
    left_ref[LM * BLOCK :, :] = filler
    right_ref[LM * BLOCK :, :] = filler


def first_moments_kernel(
    half_ref,
    count_hbm,
    rho_hbm,
    point_hbm,
    index_hbm,
    fraction_hbm,
    angular_hbm,
    out_ref,
    count_ref,
    rho_ref,
    point_ref,
    index_ref,
    fraction_ref,
    angular_ref,
    left_ref,
    right_ref,
    task_sems,
    angular_sems,
):
    first = pl.multiple_of(half_ref[0] * HALF, HALF)
    task_refs = (point_ref, index_ref, fraction_ref)

    def task_copy(n):
        source = (point_hbm, index_hbm, fraction_hbm)[n]
        return pltpu.make_async_copy(source.at[pl.ds(first, HALF), :], task_refs[n], task_sems.at[n])

    def rho_copy():
        return pltpu.make_async_copy(rho_hbm, rho_ref, task_sems.at[3])

    def count_copy():
        return pltpu.make_async_copy(count_hbm, count_ref, task_sems.at[4])

    def angular_copy(step):
        source = angular_hbm.at[:, pl.ds(first + step * BLOCK, BLOCK), :]
        return pltpu.make_async_copy(source, angular_ref.at[step], angular_sems.at[step])

    rho_copy().start()
    count_copy().start()
    for n in range(3):
        task_copy(n).start()
    for step in range(STEPS):
        angular_copy(step).start()
    fill(left_ref, right_ref)
    rho_copy().wait()
    count_copy().wait()
    for n in range(3):
        task_copy(n).wait()

    def block(step, carry):
        base = pl.multiple_of(step * BLOCK, BLOCK)

        def angular_rows():
            angular_copy(step).wait()
            return (angular_ref[step, m] for m in range(LM))

        tasks = [ref[pl.ds(base, BLOCK), :] for ref in task_refs]
        add_moments(
            base, lambda i: count_ref[0, first + base + i], tasks, angular_rows, rho_ref, out_ref, left_ref, right_ref
        )
        return carry

    lax.fori_loop(0, STEPS, block, 0)


def moments_kernel(
    half_ref, count_ref, rho_ref, point_ref, index_ref, fraction_ref, angular_ref, out_ref, left_ref, right_ref
):
    first = pl.multiple_of(half_ref[0] * HALF, HALF)
    fill(left_ref, right_ref)

    def block(step, carry):
        base = pl.multiple_of(step * BLOCK, BLOCK)
        start = pl.multiple_of(first + base, BLOCK)
        tasks = [ref[pl.ds(start, BLOCK), :] for ref in (point_ref, index_ref, fraction_ref)]
        add_moments(
            base,
            lambda i: count_ref[0, start + i],
            tasks,
            lambda: (angular_ref[m, pl.ds(start, BLOCK), :] for m in range(LM)),
            rho_ref,
            out_ref,
            left_ref,
            right_ref,
        )
        return carry

    lax.fori_loop(0, STEPS, block, 0)


def evaluate_kernel(
    half_ref, count_ref, table_ref, point_ref, index_ref, fraction_ref, angular_ref, *refs
):
    *before_ref, out_ref, left_ref, right_ref = refs
    first = pl.multiple_of(half_ref[0] * HALF, HALF)
    slot = lax.broadcasted_iota(jnp.int32, (1, SLOTS), 1)
    grid = radial_grid()

    def block(step, total):
        base = pl.multiple_of(step * BLOCK, BLOCK)
        start = pl.multiple_of(first + base, BLOCK)
        points = point_ref[pl.ds(start, BLOCK), :]
        index = index_ref[pl.ds(start, BLOCK), :]
        fraction = fraction_ref[pl.ds(start, BLOCK), :]
        for i in range(BLOCK):
            rows = hat_rows(grid, index[i : i + 1, :], fraction[i : i + 1, :])
            radial = jnp.dot(table_ref[base + i], rows, preferred_element_type=f32)
            of_atom = pl.ds(i, ROWS, stride=BLOCK)
            left_ref[of_atom, :] = radial[:, :LANES]
            right_ref[of_atom, :] = radial[:, LANES:]
        values = []
        for n, radial_ref in enumerate((left_ref, right_ref)):
            sums = [jnp.zeros((BLOCK, LANES), f32)] * 2
            for m in range(LM):
                angular = angular_ref[m, pl.ds(start, BLOCK), n * LANES : (n + 1) * LANES].astype(f32)
                sums[m % 2] = sums[m % 2] + angular * radial_ref[m * BLOCK : (m + 1) * BLOCK, :]
            values.append(sums[0] + sums[1])
        values = jnp.concatenate(values, axis=1)
        for i in range(BLOCK):
            value = jnp.where(slot < count_ref[0, start + i], values[i : i + 1, :], 0.0)
            big = value.astype(bf16).astype(f32)
            small = value - big
            high = is_high(points[i : i + 1, :])
            spread = jnp.concatenate([jnp.where(high, big, 0.0), jnp.where(high, small, 0.0)], axis=0)
            low = one_hot_low(grid, points[i : i + 1, :])
            total = total + lax.dot_general(
                spread.astype(bf16), low, (((1,), (1,)), ((), ())), preferred_element_type=f32
            )
        return total

    total = lax.fori_loop(0, STEPS, block, jnp.zeros((2 * HIGH, LOW), f32))
    total = total[:HIGH] + total[HIGH:]
    out_ref[...] = total + before_ref[0][...] if before_ref else total


def sum_kernel(arrived_ref, out_ref):
    for n in range(BLOCKS):
        plane = jnp.sum(arrived_ref[:, n].astype(f32), axis=0).astype(bf16)
        out_ref[:, n] = jnp.broadcast_to(plane, (BLOCKS, ROWS, R))


def solve_kernel(parts_ref, green_ref, table_ref):
    moments = jnp.sum(parts_ref[...].astype(f32), axis=0)
    tiles = [jnp.zeros((BLOCKS, 8, R), f32)] * (ROWS // 8)
    for degree in range(LMAX + 1):
        start, stop = degree * degree, (degree + 1) * (degree + 1)
        first, last = start // 8, (stop - 1) // 8 + 1
        count = (last - first) * 8
        row = lax.broadcasted_iota(jnp.int32, (BLOCKS, count, R), 1) + first * 8
        of_degree = jnp.where((row >= start) & (row < stop), moments[:, first * 8 : last * 8], 0.0)
        solved = jnp.dot(
            of_degree.reshape(BLOCKS * count, R),
            green_ref[degree],
            precision=lax.Precision.HIGHEST,
            preferred_element_type=f32,
        ).reshape(BLOCKS, count, R)
        for tile in range(first, last):
            tiles[tile] = tiles[tile] + solved[:, (tile - first) * 8 : (tile - first + 1) * 8]
    table_ref[...] = jnp.concatenate(tiles, axis=1).astype(bf16)


def join_kernel(part_ref, own_ref, below_ref, above_ref, out_ref):
    part = part_ref[0]
    places = (part, jnp.where(part == 0, PARTS - 1, part - 1), jnp.where(part == PARTS - 1, 0, part + 1))
    for place, tables_ref in zip(places, (own_ref, below_ref, above_ref)):
        for n in range(X):
            out_ref[n, place] = tables_ref[...]


VMEM = pl.BlockSpec(memory_space=pltpu.VMEM)
SMEM = pl.BlockSpec(memory_space=pltpu.SMEM)
HBM = pl.BlockSpec(memory_space=pltpu.HBM)
GRANT = pltpu.CompilerParams(vmem_limit_bytes=16 << 20)


def first_moments_of(half, count, rho, points, index, fraction, angular):
    return pl.pallas_call(
        first_moments_kernel,
        out_shape=pltpu.VMEM((HALF, ROWS, R), bf16),
        in_specs=[SMEM] + [HBM] * 6,
        out_specs=VMEM,
        scratch_shapes=[
            pltpu.SMEM((1, 2 * HALF), jnp.int32),
            pltpu.VMEM((HIGH, LOW), f32),
            pltpu.VMEM((HALF, SLOTS), jnp.int32),
            pltpu.VMEM((HALF, SLOTS), jnp.int32),
            pltpu.VMEM((HALF, SLOTS), f32),
            pltpu.VMEM((STEPS, LM, BLOCK, SLOTS), bf16),
            pltpu.VMEM((ROWS * BLOCK, LANES), f32),
            pltpu.VMEM((ROWS * BLOCK, LANES), f32),
            pltpu.SemaphoreType.DMA((5,)),
            pltpu.SemaphoreType.DMA((STEPS,)),
        ],
        compiler_params=GRANT,
        name="first_moments",
    )(half, count, rho, points, index, fraction, angular)


def moments_of(half, count, rho, points, index, fraction, angular):
    return pl.pallas_call(
        moments_kernel,
        out_shape=pltpu.VMEM((HALF, ROWS, R), f32),
        in_specs=[SMEM, SMEM] + [VMEM] * 5,
        out_specs=VMEM,
        scratch_shapes=[pltpu.VMEM((ROWS * BLOCK, LANES), f32)] * 2,
        compiler_params=GRANT,
        name="moments",
    )(half, count, rho, points, index, fraction, angular)


def evaluated(half, count, table, points, index, fraction, angular, *before):
    return pl.pallas_call(
        evaluate_kernel,
        out_shape=pltpu.VMEM((HIGH, LOW), f32),
        in_specs=[SMEM, SMEM] + [VMEM] * (5 + len(before)),
        out_specs=VMEM,
        scratch_shapes=[pltpu.VMEM((ROWS * BLOCK, LANES), f32)] * 2,
        compiler_params=GRANT,
        name="evaluate",
    )(half, count, table, points, index, fraction, angular, *before)


def summed(arrived):
    return pl.pallas_call(
        sum_kernel,
        out_shape=pltpu.VMEM((BLOCKS, BLOCKS, ROWS, R), bf16),
        in_specs=[VMEM],
        out_specs=VMEM,
        compiler_params=GRANT,
        name="sum",
    )(arrived)


def solved(parts, green):
    return pl.pallas_call(
        solve_kernel,
        out_shape=pltpu.VMEM((BLOCKS, ROWS, R), bf16),
        in_specs=[VMEM, VMEM],
        out_specs=VMEM,
        compiler_params=GRANT,
        name="solve",
    )(parts, green)


def joined(part, own, below, above):
    return pl.pallas_call(
        join_kernel,
        out_shape=pltpu.VMEM((X, PARTS, BLOCKS, ROWS, R), bf16),
        in_specs=[SMEM] + [VMEM] * 3,
        out_specs=VMEM,
        compiler_params=GRANT,
        name="join",
    )(part, own, below, above)


def along_z(array, step):
    count = BLOCKS * PARTS
    return lax.ppermute(array, ("block", "part"), [(z, (z + step) % count) for z in range(count)])


def exchanged(array, axis):
    return lax.all_to_all(array, axis, split_axis=0, concat_axis=0, tiled=True)


def to_other_core(array):
    return lax.ppermute(array, "core", [(0, 1), (1, 0)])


def far(array):
    return pltpu.with_memory_space_constraint(array, pltpu.HBM)


def near(array):
    return pltpu.with_memory_space_constraint(array, pltpu.VMEM)


def per_device(rho, task_point, task_count, radial_index, fraction, angular, green):
    core = lax.axis_index("core")
    own = core.astype(jnp.int32).reshape(1)
    other = 1 - own
    tasks = (task_point[0], radial_index[0], fraction[0], angular[0].transpose(1, 0, 2))
    count = task_count
    rho = rho.reshape(HIGH, LOW)

    sent = first_moments_of(other, *(far(array) for array in (count, rho, *tasks)))
    arrived = to_other_core(sent)
    tasks = [near(array) for array in tasks]
    kept = moments_of(own, count, near(rho), *tasks)
    chip = (kept + arrived.astype(f32)).astype(bf16)
    arrived = exchanged(chip.reshape(IN_BLOCK, BLOCKS, ROWS, R), ("x", "part"))
    parts = exchanged(summed(near(arrived)), "block")
    tables = solved(near(parts), near(green))
    part = lax.axis_index("part").astype(jnp.int32).reshape(1)
    column = joined(part, tables, along_z(tables, 1), along_z(tables, -1))
    half = exchanged(column, "x").reshape(HALF, ROWS, R)
    other_half = to_other_core(half)
    terms = evaluated(own, count, near(half), *tasks)
    terms = evaluated(other, count, near(other_half), *tasks, terms)
    return exchanged(terms.reshape(8, PTS // 8), "atom").sum(axis=0)


def solution(mesh):
    mesh = Mesh(mesh.devices.reshape(X, BLOCKS, PARTS, CORES, 8), ("x", "block", "part", "core", "atom"))
    shell = ("x", "block", "part", "core")
    in_specs = (
        P(shell),
        P(shell, "atom", None),
        P(shell, "atom"),
        P(shell, "atom", None),
        P(shell, "atom", None),
        P(shell, "atom", None, None),
        P(),
    )
    return jax.shard_map(
        per_device, mesh=mesh, in_specs=in_specs, out_specs=P((*shell, "atom")), check_vma=False
    )
```

```python
import jax
import jax.numpy as jnp
from jax import lax
from jax.experimental import pallas as pl
from jax.experimental.pallas import tpu as pltpu
from jax.sharding import Mesh, PartitionSpec as P

X, BLOCKS, PARTS, CORES = 4, 4, 3, 2
IN_BLOCK = X * PARTS
LMAX = 6
LM = 49
ROWS = 56
R = 128
SLOTS = 256
LANES = 128
PTS = 4096
HALF = IN_BLOCK * BLOCKS
BLOCK = 24
STEPS = HALF // BLOCK
HIGH, LOW = 32, 128
TILE = 16

f32 = jnp.float32
bf16 = jnp.bfloat16


def radial_grid():
    shape = (R // TILE, TILE, SLOTS)
    grid = lax.broadcasted_iota(jnp.int32, shape, 0) * TILE + lax.broadcasted_iota(jnp.int32, shape, 1)
    return grid.astype(f32).astype(bf16)


def tile_of(row):
    return jnp.broadcast_to(row, (TILE, SLOTS)).astype(bf16)[None]


def hat_parts(index, fraction):
    index = index.astype(f32)
    return index, index + 1.0, fraction, 1.0 - fraction


def hat_rows(grid, parts, i):
    index, following, fraction, rest = (tile_of(part[i : i + 1, :]) for part in parts)
    upper = jnp.where(grid == following, fraction, jnp.zeros((), bf16))
    return jnp.where(grid == index, rest, upper).reshape(R, SLOTS)


def one_hot_low(grid, low, i):
    same = grid == tile_of(low[i : i + 1, :])
    return jnp.where(same, jnp.ones((), bf16), jnp.zeros((), bf16)).reshape(LOW, SLOTS)


def low_of(points):
    return (points & (LOW - 1)).astype(f32)


def high_of(points):
    return lax.shift_right_logical(points, 7)


def add_moments(base, counts, tasks, angular_rows, rho_ref, out_ref, left_ref, right_ref):
    points, index, fraction = tasks
    rho = rho_ref[...]
    big = rho.astype(bf16)
    small = (rho - big.astype(f32)).astype(bf16)
    rho_parts = jnp.concatenate([big, small], axis=1)
    slot = lax.broadcasted_iota(jnp.int32, (1, SLOTS), 1)
    grid = radial_grid()
    densities = []
    lows, highs = low_of(points), high_of(points)
    parts = hat_parts(index, fraction)
    high_grid = lax.broadcasted_iota(jnp.int32, (HIGH, SLOTS), 0)
    for i in range(BLOCK):
        low = one_hot_low(grid, lows, i)
        columns = jnp.dot(rho_parts, jnp.concatenate([low, low], axis=0), preferred_element_type=f32)
        picked = jnp.sum(jnp.where(high_grid == highs[i : i + 1, :], columns, 0.0), axis=0, keepdims=True)
        densities.append(jnp.where(slot < counts(i), picked, 0.0))
    densities = jnp.concatenate(densities, axis=0)
    for m, angular in enumerate(angular_rows()):
        weighted = angular.astype(f32) * densities
        left_ref[m * BLOCK : (m + 1) * BLOCK, :] = weighted[:, :LANES]
        right_ref[m * BLOCK : (m + 1) * BLOCK, :] = weighted[:, LANES:]
    for i in range(BLOCK):
        of_atom = pl.ds(i, ROWS, stride=BLOCK)
        weighted = jnp.concatenate([left_ref[of_atom, :], right_ref[of_atom, :]], axis=1).astype(bf16)
        rows = hat_rows(grid, parts, i)
        out_ref[base + i] = lax.dot_general(
            weighted, rows, (((1,), (1,)), ((), ())), preferred_element_type=f32
        ).astype(out_ref.dtype)


def fill(left_ref, right_ref):
    filler = jnp.zeros(((ROWS - LM) * BLOCK, LANES), f32)
    left_ref[LM * BLOCK :, :] = filler
    right_ref[LM * BLOCK :, :] = filler


def first_moments_kernel(
    half_ref,
    count_hbm,
    rho_hbm,
    point_hbm,
    index_hbm,
    fraction_hbm,
    angular_hbm,
    out_ref,
    count_ref,
    rho_ref,
    point_ref,
    index_ref,
    fraction_ref,
    angular_ref,
    left_ref,
    right_ref,
    task_sems,
    angular_sems,
):
    first = pl.multiple_of(half_ref[0] * HALF, HALF)
    task_refs = (point_ref, index_ref, fraction_ref)

    def task_copy(n):
        source = (point_hbm, index_hbm, fraction_hbm)[n]
        return pltpu.make_async_copy(source.at[pl.ds(first, HALF), :], task_refs[n], task_sems.at[n])

    def rho_copy():
        return pltpu.make_async_copy(rho_hbm, rho_ref, task_sems.at[3])

    def count_copy():
        return pltpu.make_async_copy(count_hbm, count_ref, task_sems.at[4])

    def angular_copy(step):
        source = angular_hbm.at[:, pl.ds(first + step * BLOCK, BLOCK), :]
        return pltpu.make_async_copy(source, angular_ref.at[step], angular_sems.at[step])

    rho_copy().start()
    count_copy().start()
    for n in range(3):
        task_copy(n).start()
    for step in range(STEPS):
        angular_copy(step).start()
    fill(left_ref, right_ref)
    rho_copy().wait()
    count_copy().wait()
    for n in range(3):
        task_copy(n).wait()

    def block(step, carry):
        base = pl.multiple_of(step * BLOCK, BLOCK)

        def angular_rows():
            angular_copy(step).wait()
            return (angular_ref[step, m] for m in range(LM))

        tasks = [ref[pl.ds(base, BLOCK), :] for ref in task_refs]
        add_moments(
            base, lambda i: count_ref[0, first + base + i], tasks, angular_rows, rho_ref, out_ref, left_ref, right_ref
        )
        return carry

    lax.fori_loop(0, STEPS, block, 0)


def moments_kernel(
    half_ref, count_ref, rho_ref, point_ref, index_ref, fraction_ref, angular_ref, out_ref, left_ref, right_ref
):
    first = pl.multiple_of(half_ref[0] * HALF, HALF)
    fill(left_ref, right_ref)

    def block(step, carry):
        base = pl.multiple_of(step * BLOCK, BLOCK)
        start = pl.multiple_of(first + base, BLOCK)
        tasks = [ref[pl.ds(start, BLOCK), :] for ref in (point_ref, index_ref, fraction_ref)]
        add_moments(
            base,
            lambda i: count_ref[0, start + i],
            tasks,
            lambda: (angular_ref[m, pl.ds(start, BLOCK), :] for m in range(LM)),
            rho_ref,
            out_ref,
            left_ref,
            right_ref,
        )
        return carry

    lax.fori_loop(0, STEPS, block, 0)


def evaluate_kernel(
    half_ref, count_ref, table_ref, point_ref, index_ref, fraction_ref, angular_ref, *refs
):
    *before_ref, out_ref, left_ref, right_ref = refs
    first = pl.multiple_of(half_ref[0] * HALF, HALF)
    slot = lax.broadcasted_iota(jnp.int32, (1, SLOTS), 1)
    grid = radial_grid()

    def block(step, total):
        base = pl.multiple_of(step * BLOCK, BLOCK)
        start = pl.multiple_of(first + base, BLOCK)
        points = point_ref[pl.ds(start, BLOCK), :]
        index = index_ref[pl.ds(start, BLOCK), :]
        fraction = fraction_ref[pl.ds(start, BLOCK), :]
        parts = hat_parts(index, fraction)
        for i in range(BLOCK):
            rows = hat_rows(grid, parts, i)
            radial = jnp.dot(table_ref[base + i], rows, preferred_element_type=f32)
            of_atom = pl.ds(i, ROWS, stride=BLOCK)
            left_ref[of_atom, :] = radial[:, :LANES]
            right_ref[of_atom, :] = radial[:, LANES:]
        values = []
        for n, radial_ref in enumerate((left_ref, right_ref)):
            sums = [jnp.zeros((BLOCK, LANES), f32)] * 2
            for m in range(LM):
                angular = angular_ref[m, pl.ds(start, BLOCK), n * LANES : (n + 1) * LANES].astype(f32)
                sums[m % 2] = sums[m % 2] + angular * radial_ref[m * BLOCK : (m + 1) * BLOCK, :]
            values.append(sums[0] + sums[1])
        values = jnp.concatenate(values, axis=1)
        lows, highs = low_of(points), high_of(points).astype(f32)
        bigs = values.astype(bf16).astype(f32)
        smalls = values - bigs
        none = jnp.zeros((), bf16)
        for i in range(BLOCK):
            live = slot < count_ref[0, start + i]
            big = tile_of(jnp.where(live, bigs[i : i + 1, :], 0.0))
            small = tile_of(jnp.where(live, smalls[i : i + 1, :], 0.0))
            high = grid[: HIGH // TILE] == tile_of(highs[i : i + 1, :])
            spread = jnp.concatenate([jnp.where(high, big, none), jnp.where(high, small, none)], axis=0)
            total = total + lax.dot_general(
                spread.reshape(2 * HIGH, SLOTS),
                one_hot_low(grid, lows, i),
                (((1,), (1,)), ((), ())),
                preferred_element_type=f32,
            )
        return total

    total = lax.fori_loop(0, STEPS, block, jnp.zeros((2 * HIGH, LOW), f32))
    total = total[:HIGH] + total[HIGH:]
    out_ref[...] = total + before_ref[0][...] if before_ref else total


def sum_kernel(arrived_ref, out_ref):
    for n in range(BLOCKS):
        plane = jnp.sum(arrived_ref[:, n].astype(f32), axis=0).astype(bf16)
        out_ref[:, n] = jnp.broadcast_to(plane, (BLOCKS, ROWS, R))


def solve_kernel(parts_ref, green_ref, table_ref):
    moments = jnp.sum(parts_ref[...].astype(f32), axis=0)
    tiles = [jnp.zeros((BLOCKS, 8, R), f32)] * (ROWS // 8)
    for degree in range(LMAX + 1):
        start, stop = degree * degree, (degree + 1) * (degree + 1)
        first, last = start // 8, (stop - 1) // 8 + 1
        count = (last - first) * 8
        row = lax.broadcasted_iota(jnp.int32, (BLOCKS, count, R), 1) + first * 8
        of_degree = jnp.where((row >= start) & (row < stop), moments[:, first * 8 : last * 8], 0.0)
        solved = jnp.dot(
            of_degree.reshape(BLOCKS * count, R),
            green_ref[degree],
            precision=lax.Precision.HIGHEST,
            preferred_element_type=f32,
        ).reshape(BLOCKS, count, R)
        for tile in range(first, last):
            tiles[tile] = tiles[tile] + solved[:, (tile - first) * 8 : (tile - first + 1) * 8]
    table = jnp.concatenate(tiles, axis=1).astype(bf16)
    table_ref[...] = jnp.broadcast_to(table, (IN_BLOCK, BLOCKS, ROWS, R))


VMEM = pl.BlockSpec(memory_space=pltpu.VMEM)
SMEM = pl.BlockSpec(memory_space=pltpu.SMEM)
HBM = pl.BlockSpec(memory_space=pltpu.HBM)
GRANT = pltpu.CompilerParams(vmem_limit_bytes=16 << 20)


def first_moments_of(half, count, rho, points, index, fraction, angular):
    return pl.pallas_call(
        first_moments_kernel,
        out_shape=pltpu.VMEM((HALF, ROWS, R), bf16),
        in_specs=[SMEM] + [HBM] * 6,
        out_specs=VMEM,
        scratch_shapes=[
            pltpu.SMEM((1, 2 * HALF), jnp.int32),
            pltpu.VMEM((HIGH, LOW), f32),
            pltpu.VMEM((HALF, SLOTS), jnp.int32),
            pltpu.VMEM((HALF, SLOTS), jnp.int32),
            pltpu.VMEM((HALF, SLOTS), f32),
            pltpu.VMEM((STEPS, LM, BLOCK, SLOTS), bf16),
            pltpu.VMEM((ROWS * BLOCK, LANES), f32),
            pltpu.VMEM((ROWS * BLOCK, LANES), f32),
            pltpu.SemaphoreType.DMA((5,)),
            pltpu.SemaphoreType.DMA((STEPS,)),
        ],
        compiler_params=GRANT,
        name="first_moments",
    )(half, count, rho, points, index, fraction, angular)


def moments_of(half, count, rho, points, index, fraction, angular):
    return pl.pallas_call(
        moments_kernel,
        out_shape=pltpu.VMEM((HALF, ROWS, R), f32),
        in_specs=[SMEM, SMEM] + [VMEM] * 5,
        out_specs=VMEM,
        scratch_shapes=[pltpu.VMEM((ROWS * BLOCK, LANES), f32)] * 2,
        compiler_params=GRANT,
        name="moments",
    )(half, count, rho, points, index, fraction, angular)


def evaluated(half, count, table, points, index, fraction, angular, *before):
    return pl.pallas_call(
        evaluate_kernel,
        out_shape=pltpu.VMEM((HIGH, LOW), f32),
        in_specs=[SMEM, SMEM] + [VMEM] * (5 + len(before)),
        out_specs=VMEM,
        scratch_shapes=[pltpu.VMEM((ROWS * BLOCK, LANES), f32)] * 2,
        compiler_params=GRANT,
        name="evaluate",
    )(half, count, table, points, index, fraction, angular, *before)


def summed(arrived):
    return pl.pallas_call(
        sum_kernel,
        out_shape=pltpu.VMEM((BLOCKS, BLOCKS, ROWS, R), bf16),
        in_specs=[VMEM],
        out_specs=VMEM,
        compiler_params=GRANT,
        name="sum",
    )(arrived)


def solved(parts, green):
    return pl.pallas_call(
        solve_kernel,
        out_shape=pltpu.VMEM((IN_BLOCK, BLOCKS, ROWS, R), bf16),
        in_specs=[VMEM, VMEM],
        out_specs=VMEM,
        compiler_params=GRANT,
        name="solve",
    )(parts, green)


def exchanged(array, axis):
    return lax.all_to_all(array, axis, split_axis=0, concat_axis=0, tiled=True)


def to_other_core(array):
    return lax.ppermute(array, "core", [(0, 1), (1, 0)])


def far(array):
    return pltpu.with_memory_space_constraint(array, pltpu.HBM)


def near(array):
    return pltpu.with_memory_space_constraint(array, pltpu.VMEM)


def per_device(rho, task_point, task_count, radial_index, fraction, angular, green):
    core = lax.axis_index("core")
    own = core.astype(jnp.int32).reshape(1)
    other = 1 - own
    tasks = (task_point[0], radial_index[0], fraction[0], angular[0].transpose(1, 0, 2))
    count = task_count
    rho = rho.reshape(HIGH, LOW)

    sent = first_moments_of(other, *(far(array) for array in (count, rho, *tasks)))
    arrived = to_other_core(sent)
    tasks = [near(array) for array in tasks]
    kept = moments_of(own, count, near(rho), *tasks)
    chip = (kept + arrived.astype(f32)).astype(bf16)
    arrived = exchanged(chip.reshape(IN_BLOCK, BLOCKS, ROWS, R), ("x", "part"))
    parts = exchanged(summed(near(arrived)), "block")
    half = exchanged(solved(near(parts), near(green)), ("x", "part")).reshape(HALF, ROWS, R)
    other_half = to_other_core(half)
    terms = evaluated(own, count, near(half), *tasks)
    terms = evaluated(other, count, near(other_half), *tasks, terms)
    return exchanged(terms.reshape(8, PTS // 8), "atom").sum(axis=0)


def solution(mesh):
    mesh = Mesh(mesh.devices.reshape(X, BLOCKS, PARTS, CORES, 8), ("x", "block", "part", "core", "atom"))
    shell = ("x", "block", "part", "core")
    in_specs = (
        P(shell),
        P(shell, "atom", None),
        P(shell, "atom"),
        P(shell, "atom", None),
        P(shell, "atom", None),
        P(shell, "atom", None, None),
        P(),
    )
    return jax.shard_map(
        per_device, mesh=mesh, in_specs=in_specs, out_specs=P((*shell, "atom")), check_vma=False
    )
```
